512 devices in a mesh: dp: 32 (over y_lo, z), mp: 16 (over x, y_hi, core).
Axes of the slice: x: 4, y: 8 (y_hi: 2, y_lo: 4; y = y_hi * 4 + y_lo), z: 8, core: 2. Of those that a mesh axis runs over, the one named last changes fastest.
Arguments:
- queries: bfloat16 [4096, 4096], P('dp', 'mp'), may hold values from -64 to 64
- database: bfloat16 [16384, 896], P('dp'), may hold values from -9 to 9
- key_weight: bfloat16 [896, 4096], P(None, 'mp'), may hold values from -1 to 2
- value_weight: bfloat16 [896, 4096], P(None, 'mp'), may hold values from -0.1875 to 0.1875
- out_weight: bfloat16 [4096, 8192], P('mp', 'dp'), may hold values from -0.1875 to 0.1875
- neighbours: int32 [64, 2], P('dp'), may hold values from 0 to 127, as said below
Outputs:
- mixed: bfloat16 [4096, 8192], P('dp', 'mp')
The draws below stay inside these ranges and needn't reach their ends.
Inputs may be any that keep to these rules, and one draw needn't show every extreme that they name: neighbours[c, n] names block neighbours[c, n] % 4 of database shard neighbours[c, n] // 4; among the 4 neighbours of the spans 2 * i to 2 * i + 1, no two lie in the same shard.
All inputs are finite; a program needn't handle non-finite values.
Results may differ from the reference program's by a relative error of at most 0.018.
Values may be sent and summed in bfloat16 or wider, within the bound.
No kernel may reach another device: no remote copies, remote signals or barrier semaphores. Data moves between devices by JAX's collectives and lax.ppermute only.
A program may use at most 64 MiB of HBM per device.

```python
import math
import jax
import jax.numpy as jnp
from jax import lax

D = 8192
HEAD_DIM = 128
HEAD_DEV = 2
ENC_WIDTH = 896
SPAN = 64
NEIGH = 2
NROW = 128
CH_DEV = 2
BLK_DEV = 4
HEADS = 32
SHARDS = 32
SPANS = 64
TOKENS = 4096
DB_BLOCKS = 128
DB_ROWS = 16384
N_MP = 16


def draw_queries(key, part):
    inner_width = HEADS * HEAD_DIM
    values = jnp.clip(jax.random.normal(jax.random.fold_in(key, 1), (TOKENS, inner_width), jnp.float32), -6.0, 6.0)
    return values.astype(jnp.bfloat16)


def draw_database(key, part):
    values = jnp.clip(jax.random.normal(jax.random.fold_in(key, 5), (DB_ROWS, ENC_WIDTH), jnp.float32), -6.0, 6.0)
    return values.astype(jnp.bfloat16)


def draw_key_weight(key, part):
    inner_width = HEADS * HEAD_DIM
    values = jnp.clip(jax.random.normal(jax.random.fold_in(key, 7), (ENC_WIDTH, inner_width), jnp.float32), -6.0, 6.0)
    values = values / jnp.sqrt(jnp.float32(ENC_WIDTH))
    return values.astype(jnp.bfloat16)


def draw_neighbours(key, part):
    picks = CH_DEV * NEIGH
    half_shard = SHARDS // 2
    popular = jax.random.randint(jax.random.fold_in(key, 21), (SHARDS,), 0, 4)
    noise = jax.random.randint(jax.random.fold_in(key, 22), (SHARDS, SHARDS), 0, 65536)
    ranking = (popular[None, :] * 16384 + noise) * SHARDS + jnp.arange(SHARDS, dtype=jnp.int32)[None, :]
    row_ids = jnp.arange(SHARDS, dtype=jnp.int32)[:, None]
    col_ids = jnp.arange(SHARDS, dtype=jnp.int32)[None, :]
    favoured = (row_ids == 0) & (col_ids == half_shard)
    avoided = ((row_ids == 1) | (row_ids == SHARDS - 1)) & (col_ids == half_shard)
    ranking = ranking + jnp.where(favoured, 1 << 26, 0) - jnp.where(avoided, 1 << 26, 0)
    chosen = lax.top_k(ranking, picks)[1].astype(jnp.int32)
    shuffle = jax.random.randint(jax.random.fold_in(key, 23), (SHARDS, picks), 0, 65536) * picks
    shuffle = shuffle + jnp.arange(picks, dtype=jnp.int32)[None, :]
    order = jnp.argsort(shuffle, axis=1, stable=True)
    chosen = jnp.take_along_axis(chosen, order, axis=1)
    inside = jax.random.randint(jax.random.fold_in(key, 24), (SHARDS, picks), 0, BLK_DEV)
    forced = (row_ids == 0) & (chosen == half_shard)
    inside = jnp.where(forced, BLK_DEV - 1, inside)
    block_ids = chosen * BLK_DEV + inside
    return block_ids.reshape(SPANS, NEIGH).astype(jnp.int32)


def with_spikes(array, own_key, source, target, shards_of, factor):
    owner, partner = [(jnp.arange(array.shape[axis_at]) // (array.shape[axis_at] // shards_of)).reshape([-1 if axis == axis_at else 1 for axis in range(array.ndim)]) for axis_at in (source, target)]
    chosen = jax.random.permutation(own_key, shards_of)[partner]
    strong = (owner == chosen) | (owner == (partner + shards_of // 2) % shards_of)
    return jnp.where(strong, factor * array, array)


def levels(rng, shape, pieces, least, high):
    gain = 1.0
    for dim, parts in pieces:
        draws = jax.random.uniform(jax.random.fold_in(jax.random.fold_in(rng, 6), dim), (parts,), jnp.float32, least / len(pieces), high / len(pieces))
        gain = gain * jnp.repeat(jnp.exp(draws), shape[dim] // parts).reshape((-1,) + (1,) * (len(shape) - 1 - dim))
    return gain


def normal_values(own_key, extent, deviation, most, shards=(), kind=jnp.bfloat16):
    array = jax.random.normal(own_key, extent, jnp.float32) * deviation
    if len(shards) > 0:
        array = levels(own_key, extent, shards, -0.22, 0.18) * array
    return jnp.clip(array, min=-most, max=most).astype(kind)


def bell_draw_with(own_key, extent, deviation, most, shards, heavy, kind=jnp.bfloat16):
    array = deviation * jax.random.normal(own_key, extent, jnp.float32)
    if shards:
        array = array * levels(own_key, extent, shards, -0.22, 0.18)
    return jnp.clip(with_spikes(array, jax.random.fold_in(own_key, 3), *heavy), -most, most).astype(kind)


def setup_inputs(seed: int = 0) -> dict:
    splits = jax.random.split(jax.random.key(seed), 7)
    return {
        "queries": draw_queries(jax.random.fold_in(splits[6], 71), 0),
        "database": draw_database(jax.random.fold_in(splits[6], 71), 0),
        "key_weight": draw_key_weight(jax.random.fold_in(splits[6], 71), 0),
        "value_weight": normal_values(splits[3], (ENC_WIDTH, HEADS * HEAD_DIM), ENC_WIDTH ** -0.5, 0.1875, ((1, 16),)),
        "out_weight": bell_draw_with(splits[4], (HEADS * HEAD_DIM, D), (HEADS * HEAD_DIM) ** -0.5, 0.1875, ((0, 16), (1, 32)), (0, 1, 32, 2.75)),
        "neighbours": draw_neighbours(jax.random.fold_in(splits[6], 71), 0),
    }


def reference(queries, database, key_weight, value_weight, out_weight, neighbours):
    inner_width = HEADS * HEAD_DIM
    keys_all = jnp.dot(database, key_weight, preferred_element_type=jnp.float32).astype(jnp.bfloat16)
    values_all = jnp.dot(database, value_weight, preferred_element_type=jnp.float32).astype(jnp.bfloat16)
    keys_all = keys_all.reshape(DB_BLOCKS, NROW, inner_width)
    values_all = values_all.reshape(DB_BLOCKS, NROW, inner_width)
    flat_ids = neighbours.reshape(-1).astype(jnp.int32)
    near_keys = keys_all[flat_ids].reshape(SPANS, NEIGH * NROW, HEADS, HEAD_DIM).astype(jnp.float32)
    near_values = values_all[flat_ids].reshape(SPANS, NEIGH * NROW, HEADS, HEAD_DIM).astype(jnp.float32)
    query_blocks = queries.reshape(SPANS, SPAN, HEADS, HEAD_DIM).astype(jnp.float32)
    scores = jnp.einsum('cqhd,ckhd->chqk', query_blocks, near_keys) / math.sqrt(HEAD_DIM)
    weights = jax.nn.softmax(scores, axis=-1).astype(jnp.bfloat16)
    weights = lax.optimization_barrier(weights).astype(jnp.float32)
    attended = jnp.einsum('chqk,ckhd->cqhd', weights, near_values).astype(jnp.bfloat16)
    attended = attended.reshape(TOKENS, inner_width)
    group_width = HEAD_DEV * HEAD_DIM

    def add_group(running, group_index):
        offset = (group_index * group_width).astype(jnp.int32)
        columns = lax.dynamic_slice_in_dim(attended, offset, group_width, 1)
        weight_rows = lax.dynamic_slice_in_dim(out_weight, offset, group_width, 0)
        part_sum = jnp.dot(columns, weight_rows, preferred_element_type=jnp.float32).astype(jnp.bfloat16)
        part_sum = lax.optimization_barrier(part_sum)
        return (running + part_sum.astype(jnp.float32), None)
    running, _ = lax.scan(add_group, jnp.zeros((TOKENS, D), jnp.float32), jnp.arange(N_MP, dtype=jnp.int32))
    return running.astype(jnp.bfloat16)
```

```python
import math

import jax
import jax.numpy as jnp
from jax import lax
from jax.sharding import PartitionSpec as P

HEAD_DIM = 128
SPAN = 64
NEIGH = 2
NROW = 128
BLK_DEV = 4


def weight_blocks(out_weight):
    dp_count = lax.axis_size("dp")
    mp_count = lax.axis_size("mp")
    ratio = dp_count // mp_count
    moves = []
    for d in range(dp_count):
        for m in range(mp_count):
            target = ((d % ratio) * mp_count + m) * mp_count + d // ratio
            moves.append((d * mp_count + m, target))
    return lax.ppermute(out_weight, ("dp", "mp"), moves)


def weight_columns(moved):
    gathered = lax.all_gather(moved, "dp", axis=0, tiled=True)
    mp_count = lax.axis_size("mp")
    return gathered.reshape(-1, mp_count * moved.shape[0], moved.shape[1])


def near_rows(database, neighbours):
    dp_count = lax.axis_size("dp")
    mp_count = lax.axis_size("mp")
    own_shard = lax.axis_index("dp")
    part = lax.axis_index("mp")
    part_rows = NROW // mp_count
    enc_width = database.shape[1]
    per_owner = neighbours.size
    ids = lax.all_gather(neighbours, "dp", axis=0, tiled=True).reshape(dp_count, per_owner)
    mine = ids // BLK_DEV == own_shard
    wanted = jnp.sum(jnp.where(mine, ids % BLK_DEV, 0), axis=1).reshape(dp_count, 1, 1)
    stored = lax.dynamic_slice(
        database.reshape(BLK_DEV, NROW, enc_width),
        (0, part * part_rows, 0),
        (BLK_DEV, part_rows, enc_width),
    )
    outgoing = stored[0][None]
    for block in range(1, BLK_DEV):
        outgoing = jnp.where(wanted == block, stored[block][None], outgoing)
    outgoing = jnp.broadcast_to(outgoing, (dp_count, part_rows, enc_width))
    arrived = lax.all_to_all(outgoing, "dp", split_axis=0, concat_axis=0, tiled=True)
    shard_of = neighbours.reshape(-1) // BLK_DEV
    chosen = [
        lax.dynamic_slice(arrived, (shard_of[j], 0, 0), (1, part_rows, enc_width))
        for j in range(per_owner)
    ]
    chosen = jnp.concatenate(chosen, axis=0)
    gathered = lax.all_gather(chosen, "mp", axis=0)
    gathered = gathered.reshape(mp_count, per_owner // NEIGH, NEIGH * part_rows, enc_width)
    return gathered.transpose(1, 0, 2, 3).reshape(-1, enc_width)


def on_device(queries, database, key_weight, value_weight, out_weight, neighbours):
    span_count = neighbours.shape[0]
    inner_width = key_weight.shape[1]
    head_count = inner_width // HEAD_DIM
    moved = weight_blocks(out_weight)
    database, moved = lax.optimization_barrier((database, moved))
    columns = weight_columns(moved)
    encoded_rows = near_rows(database, neighbours)
    near_keys = jnp.dot(encoded_rows, key_weight, preferred_element_type=jnp.float32).astype(
        jnp.bfloat16
    )
    near_values = jnp.dot(encoded_rows, value_weight, preferred_element_type=jnp.float32).astype(
        jnp.bfloat16
    )
    key_blocks = near_keys.reshape(span_count, NEIGH * NROW, head_count, HEAD_DIM)
    value_blocks = near_values.reshape(span_count, NEIGH * NROW, head_count, HEAD_DIM)
    query_blocks = queries.reshape(span_count, SPAN, head_count, HEAD_DIM)
    scores = jnp.einsum(
        "cqhd,ckhd->chqk", query_blocks, key_blocks, preferred_element_type=jnp.float32
    )
    scores = scores / math.sqrt(HEAD_DIM)
    weights = jax.nn.softmax(scores, axis=-1).astype(jnp.bfloat16)
    attended = jnp.einsum(
        "chqk,ckhd->cqhd", weights, value_blocks, preferred_element_type=jnp.float32
    )
    attended = attended.astype(jnp.bfloat16).reshape(span_count * SPAN, inner_width)
    attended, columns = lax.optimization_barrier((attended, columns))
    attended = lax.all_gather(attended, "mp", axis=1, tiled=True)
    parts = [
        jnp.dot(attended, columns[k], preferred_element_type=jnp.float32)
        for k in range(columns.shape[0])
    ]
    return jnp.concatenate(parts, axis=1).astype(jnp.bfloat16)


def solution(mesh):
    in_specs = (
        P("dp", "mp"),
        P("dp", None),
        P(None, "mp"),
        P(None, "mp"),
        P("mp", "dp"),
        P("dp", None),
    )
    out_specs = P("dp", "mp")
    return jax.shard_map(
        on_device, mesh=mesh, in_specs=in_specs, out_specs=out_specs, check_vma=False
    )
```

```python
import math

import jax
import jax.numpy as jnp
from jax import lax
from jax.sharding import PartitionSpec as P

HEAD_DIM = 128
SPAN = 64
NEIGH = 2
NROW = 128
BLK_DEV = 4


def weight_blocks(out_weight):
    dp_count = lax.axis_size("dp")
    mp_count = lax.axis_size("mp")
    ratio = dp_count // mp_count
    moves = []
    for d in range(dp_count):
        for m in range(mp_count):
            target = ((d % ratio) * mp_count + m) * mp_count + d // ratio
            moves.append((d * mp_count + m, target))
    return lax.ppermute(out_weight, ("dp", "mp"), moves)


def weight_columns(moved):
    gathered = lax.all_gather(moved, "dp", axis=0, tiled=True)
    mp_count = lax.axis_size("mp")
    return gathered.reshape(-1, mp_count * moved.shape[0], moved.shape[1])


def copies_to_all(block, axis):
    count = lax.axis_size(axis)
    copies = jnp.broadcast_to(block[None], (count, *block.shape))
    return lax.all_to_all(copies, axis, split_axis=0, concat_axis=0, tiled=True)


def near_rows(database, neighbours):
    dp_count = lax.axis_size("dp")
    mp_count = lax.axis_size("mp")
    part = lax.axis_index("mp")
    part_rows = NROW // mp_count
    enc_width = database.shape[1]
    per_owner = neighbours.size
    flat_ids = neighbours.reshape(1, per_owner)
    shard_ids = jnp.arange(dp_count, dtype=jnp.int32)[:, None]
    asked = jnp.sum(jnp.where(flat_ids // BLK_DEV == shard_ids, flat_ids % BLK_DEV, 0), axis=1)
    wanted = lax.all_to_all(
        asked.reshape(dp_count, 1), "dp", split_axis=0, concat_axis=0, tiled=True
    ).reshape(dp_count, 1, 1)
    stored = lax.dynamic_slice(
        database.reshape(BLK_DEV, NROW, enc_width),
        (0, part * part_rows, 0),
        (BLK_DEV, part_rows, enc_width),
    )
    outgoing = stored[0][None]
    for block in range(1, BLK_DEV):
        outgoing = jnp.where(wanted == block, stored[block][None], outgoing)
    outgoing = jnp.broadcast_to(outgoing, (dp_count, part_rows, enc_width))
    arrived = lax.all_to_all(outgoing, "dp", split_axis=0, concat_axis=0, tiled=True)
    shard_of = neighbours.reshape(-1) // BLK_DEV
    chosen = [
        lax.dynamic_slice(arrived, (shard_of[j], 0, 0), (1, part_rows, enc_width))
        for j in range(per_owner)
    ]
    chosen = jnp.concatenate(chosen, axis=0)
    gathered = copies_to_all(chosen, "mp")
    gathered = gathered.reshape(mp_count, per_owner // NEIGH, NEIGH * part_rows, enc_width)
    return gathered.transpose(1, 0, 2, 3).reshape(-1, enc_width)


def on_device(queries, database, key_weight, value_weight, out_weight, neighbours):
    span_count = neighbours.shape[0]
    inner_width = key_weight.shape[1]
    head_count = inner_width // HEAD_DIM
    moved = weight_blocks(out_weight)
    database, moved = lax.optimization_barrier((database, moved))
    columns = weight_columns(moved)
    encoded_rows = near_rows(database, neighbours)
    near_keys = jnp.dot(encoded_rows, key_weight, preferred_element_type=jnp.float32).astype(
        jnp.bfloat16
    )
    near_values = jnp.dot(encoded_rows, value_weight, preferred_element_type=jnp.float32).astype(
        jnp.bfloat16
    )
    key_blocks = near_keys.reshape(span_count, NEIGH * NROW, head_count, HEAD_DIM)
    value_blocks = near_values.reshape(span_count, NEIGH * NROW, head_count, HEAD_DIM)
    query_blocks = queries.reshape(span_count, SPAN, head_count, HEAD_DIM)
    scores = jnp.einsum(
        "cqhd,ckhd->chqk", query_blocks, key_blocks, preferred_element_type=jnp.float32
    )
    scores = scores / math.sqrt(HEAD_DIM)
    weights = jax.nn.softmax(scores, axis=-1).astype(jnp.bfloat16)
    attended = jnp.einsum(
        "chqk,ckhd->cqhd", weights, value_blocks, preferred_element_type=jnp.float32
    )
    attended = attended.astype(jnp.bfloat16).reshape(span_count * SPAN, inner_width)
    attended = copies_to_all(attended, "mp").transpose(1, 0, 2).reshape(span_count * SPAN, -1)
    parts = [
        jnp.dot(attended, columns[k], preferred_element_type=jnp.float32)
        for k in range(columns.shape[0])
    ]
    return jnp.concatenate(parts, axis=1).astype(jnp.bfloat16)


def solution(mesh):
    in_specs = (
        P("dp", "mp"),
        P("dp", None),
        P(None, "mp"),
        P(None, "mp"),
        P("mp", "dp"),
        P("dp", None),
    )
    out_specs = P("dp", "mp")
    return jax.shard_map(
        on_device, mesh=mesh, in_specs=in_specs, out_specs=out_specs, check_vma=False
    )
```

```python
import math

import jax
import jax.numpy as jnp
from jax import lax
from jax.sharding import PartitionSpec as P

HEAD_DIM = 128
SPAN = 64
NEIGH = 2
NROW = 128
BLK_DEV = 4


NEAR_DP = 8


def weight_blocks(out_weight):
    dp_count = lax.axis_size("dp")
    mp_count = lax.axis_size("mp")
    ratio = dp_count // mp_count
    far_count = dp_count // NEAR_DP
    moves = []
    for d in range(dp_count):
        for m in range(mp_count):
            order = (d % ratio) * mp_count + m
            place = (order % far_count) * NEAR_DP + order // far_count
            moves.append((d * mp_count + m, place * mp_count + d // ratio))
    return lax.ppermute(out_weight, ("dp", "mp"), moves)


def weight_columns(moved):
    dp_count = lax.axis_size("dp")
    mp_count = lax.axis_size("mp")
    far_groups = [list(range(z, dp_count, NEAR_DP)) for z in range(NEAR_DP)]
    near_groups = [list(range(y, y + NEAR_DP)) for y in range(0, dp_count, NEAR_DP)]
    far_count = dp_count // NEAR_DP
    copies = jnp.broadcast_to(moved[None], (far_count, *moved.shape))
    piece = lax.all_to_all(
        copies, "dp", split_axis=0, concat_axis=0, axis_index_groups=far_groups, tiled=True
    )
    piece = piece.reshape(-1, moved.shape[1])
    gathered = lax.all_gather(piece, "dp", axis=0, axis_index_groups=near_groups, tiled=True)
    return gathered.reshape(-1, mp_count * moved.shape[0], moved.shape[1])


def copies_to_all(block, axis):
    count = lax.axis_size(axis)
    copies = jnp.broadcast_to(block[None], (count, *block.shape))
    return lax.all_to_all(copies, axis, split_axis=0, concat_axis=0, tiled=True)


def rows_to_send(database, neighbours):
    dp_count = lax.axis_size("dp")
    mp_count = lax.axis_size("mp")
    part = lax.axis_index("mp")
    part_rows = NROW // mp_count
    enc_width = database.shape[1]
    per_owner = neighbours.size
    flat_ids = neighbours.reshape(1, per_owner)
    shard_ids = jnp.arange(dp_count, dtype=jnp.int32)[:, None]
    asked = jnp.sum(jnp.where(flat_ids // BLK_DEV == shard_ids, flat_ids % BLK_DEV, 0), axis=1)
    wanted = lax.all_to_all(
        asked.reshape(dp_count, 1), "dp", split_axis=0, concat_axis=0, tiled=True
    ).reshape(dp_count, 1, 1)
    stored = lax.dynamic_slice(
        database.reshape(BLK_DEV, NROW, enc_width),
        (0, part * part_rows, 0),
        (BLK_DEV, part_rows, enc_width),
    )
    outgoing = stored[0][None]
    for block in range(1, BLK_DEV):
        outgoing = jnp.where(wanted == block, stored[block][None], outgoing)
    return jnp.broadcast_to(outgoing, (dp_count, part_rows, enc_width))


def near_rows(outgoing, neighbours):
    mp_count = lax.axis_size("mp")
    dp_count, part_rows, enc_width = outgoing.shape
    per_owner = neighbours.size
    arrived = lax.all_to_all(outgoing, "dp", split_axis=0, concat_axis=0, tiled=True)
    shard_of = neighbours.reshape(-1) // BLK_DEV
    chosen = [
        lax.dynamic_slice(arrived, (shard_of[j], 0, 0), (1, part_rows, enc_width))
        for j in range(per_owner)
    ]
    chosen = jnp.concatenate(chosen, axis=0)
    gathered = copies_to_all(chosen, "mp")
    gathered = gathered.reshape(mp_count, per_owner // NEIGH, NEIGH * part_rows, enc_width)
    return gathered.transpose(1, 0, 2, 3).reshape(-1, enc_width)


def on_device(queries, database, key_weight, value_weight, out_weight, neighbours):
    span_count = neighbours.shape[0]
    inner_width = key_weight.shape[1]
    head_count = inner_width // HEAD_DIM
    moved = weight_blocks(out_weight)
    outgoing = rows_to_send(database, neighbours)
    outgoing, moved = lax.optimization_barrier((outgoing, moved))
    columns = weight_columns(moved)
    encoded_rows = near_rows(outgoing, neighbours)
    near_keys = jnp.dot(encoded_rows, key_weight, preferred_element_type=jnp.float32).astype(
        jnp.bfloat16
    )
    near_values = jnp.dot(encoded_rows, value_weight, preferred_element_type=jnp.float32).astype(
        jnp.bfloat16
    )
    key_blocks = near_keys.reshape(span_count, NEIGH * NROW, head_count, HEAD_DIM)
    value_blocks = near_values.reshape(span_count, NEIGH * NROW, head_count, HEAD_DIM)
    query_blocks = queries.reshape(span_count, SPAN, head_count, HEAD_DIM)
    scores = jnp.einsum(
        "cqhd,ckhd->chqk", query_blocks, key_blocks, preferred_element_type=jnp.float32
    )
    scores = scores / math.sqrt(HEAD_DIM)
    weights = jax.nn.softmax(scores, axis=-1).astype(jnp.bfloat16)
    attended = jnp.einsum(
        "chqk,ckhd->cqhd", weights, value_blocks, preferred_element_type=jnp.float32
    )
    attended = attended.astype(jnp.bfloat16).reshape(span_count * SPAN, inner_width)
    attended = copies_to_all(attended, "mp").transpose(1, 0, 2).reshape(span_count * SPAN, -1)
    parts = [
        jnp.dot(attended, columns[k], preferred_element_type=jnp.float32)
        for k in range(columns.shape[0])
    ]
    return jnp.concatenate(parts, axis=1).astype(jnp.bfloat16)


def solution(mesh):
    in_specs = (
        P("dp", "mp"),
        P("dp", None),
        P(None, "mp"),
        P(None, "mp"),
        P("mp", "dp"),
        P("dp", None),
    )
    out_specs = P("dp", "mp")
    return jax.shard_map(
        on_device, mesh=mesh, in_specs=in_specs, out_specs=out_specs, check_vma=False
    )
```

```python
import math

import jax
import jax.numpy as jnp
from jax import lax
from jax.sharding import PartitionSpec as P

HEAD_DIM = 128
SPAN = 64
NEIGH = 2
NROW = 128
BLK_DEV = 4
NEAR_DP = 8
FAR_MP = 2


def weight_blocks(out_weight):
    dp_count = lax.axis_size("dp")
    mp_count = lax.axis_size("mp")
    ratio = dp_count // mp_count
    far_count = dp_count // NEAR_DP
    moves = []
    for d in range(dp_count):
        for m in range(mp_count):
            column = d // ratio
            other_half = (m ^ column) // FAR_MP % 2
            member = m // (2 * FAR_MP) * FAR_MP + m % FAR_MP
            order = (other_half * ratio + d % ratio) * (mp_count // 2) + member
            place = (order % far_count) * NEAR_DP + order // far_count
            moves.append((d * mp_count + m, place * mp_count + column))
    return lax.ppermute(out_weight, ("dp", "mp"), moves)


def far_piece(moved):
    dp_count = lax.axis_size("dp")
    far_count = dp_count // NEAR_DP
    far = lax.axis_index("dp") // NEAR_DP
    piece = jnp.zeros((far_count, *moved.shape), moved.dtype)
    for step in range(far_count):
        block = moved
        if step:
            block = lax.ppermute(
                moved, "dp", [(d, d ^ (step * NEAR_DP)) for d in range(dp_count)]
            )
        piece = lax.dynamic_update_slice(piece, block[None], (far ^ step, 0, 0))
    return piece.reshape(-1, moved.shape[1])


def near_gather(piece):
    dp_count = lax.axis_size("dp")
    near_groups = [list(range(y, y + NEAR_DP)) for y in range(0, dp_count, NEAR_DP)]
    return lax.all_gather(piece, "dp", axis=0, axis_index_groups=near_groups, tiled=True)


def copies_to_half(block):
    mp_count = lax.axis_size("mp")
    groups = [
        [m for m in range(mp_count) if m // FAR_MP % 2 == half] for half in range(2)
    ]
    copies = jnp.broadcast_to(block[None], (mp_count // 2, *block.shape))
    return lax.all_to_all(
        copies, "mp", split_axis=0, concat_axis=0, axis_index_groups=groups, tiled=True
    )


def copies_to_all(block):
    mp_count = lax.axis_size("mp")
    other = lax.ppermute(block, "mp", [(m, m ^ FAR_MP) for m in range(mp_count)])
    own_half = copies_to_half(block)
    other, own_half = lax.optimization_barrier((other, own_half))
    return own_half, copies_to_half(other)


def rows_to_send(database, neighbours, moved):
    dp_count = lax.axis_size("dp")
    mp_count = lax.axis_size("mp")
    part = lax.axis_index("mp")
    part_rows = NROW // mp_count
    enc_width = database.shape[1]
    per_owner = neighbours.size
    flat_ids = neighbours.reshape(1, per_owner)
    shard_ids = jnp.arange(dp_count, dtype=jnp.int32)[:, None]
    asked = jnp.sum(jnp.where(flat_ids // BLK_DEV == shard_ids, flat_ids % BLK_DEV, 0), axis=1)
    wanted = lax.all_to_all(
        asked.reshape(dp_count, 1), "dp", split_axis=0, concat_axis=0, tiled=True
    ).reshape(dp_count, 1, 1)
    stored = lax.dynamic_slice(
        database.reshape(BLK_DEV, NROW, enc_width),
        (0, part * part_rows, 0),
        (BLK_DEV, part_rows, enc_width),
    )
    outgoing = stored[0][None]
    for block in range(1, BLK_DEV):
        outgoing = jnp.where(wanted == block, stored[block][None], outgoing)
    outgoing = jnp.broadcast_to(outgoing, (dp_count, part_rows, enc_width))
    return lax.optimization_barrier((outgoing, moved))


def near_rows(arrived, neighbours):
    part_rows, enc_width = arrived.shape[1:]
    per_owner = neighbours.size
    shard_of = neighbours.reshape(-1) // BLK_DEV
    chosen = [
        lax.dynamic_slice(arrived, (shard_of[j], 0, 0), (1, part_rows, enc_width))
        for j in range(per_owner)
    ]
    chosen = jnp.concatenate(chosen, axis=0)
    halves = [
        half.reshape(-1, per_owner // NEIGH, NEIGH * part_rows, enc_width)
        for half in copies_to_all(chosen)
    ]
    gathered = jnp.concatenate(halves, axis=0)
    return gathered.transpose(1, 0, 2, 3).reshape(-1, enc_width)


def on_device(queries, database, key_weight, value_weight, out_weight, neighbours):
    span_count = neighbours.shape[0]
    inner_width = key_weight.shape[1]
    head_count = inner_width // HEAD_DIM
    tokens = span_count * SPAN
    moved = weight_blocks(out_weight)
    outgoing, moved = rows_to_send(database, neighbours, moved)
    arrived = lax.all_to_all(outgoing, "dp", split_axis=0, concat_axis=0, tiled=True)
    piece = far_piece(moved)
    arrived, piece = lax.optimization_barrier((arrived, piece))
    columns = near_gather(piece)
    encoded_rows = near_rows(arrived, neighbours)
    near_keys = jnp.dot(encoded_rows, key_weight, preferred_element_type=jnp.float32).astype(
        jnp.bfloat16
    )
    near_values = jnp.dot(encoded_rows, value_weight, preferred_element_type=jnp.float32).astype(
        jnp.bfloat16
    )
    key_blocks = near_keys.reshape(span_count, NEIGH * NROW, head_count, HEAD_DIM)
    value_blocks = near_values.reshape(span_count, NEIGH * NROW, head_count, HEAD_DIM)
    query_blocks = queries.reshape(span_count, SPAN, head_count, HEAD_DIM)
    scores = jnp.einsum(
        "cqhd,ckhd->chqk", query_blocks, key_blocks, preferred_element_type=jnp.float32
    )
    scores = scores / math.sqrt(HEAD_DIM)
    weights = jax.nn.softmax(scores, axis=-1).astype(jnp.bfloat16)
    attended = jnp.einsum(
        "chqk,ckhd->cqhd", weights, value_blocks, preferred_element_type=jnp.float32
    )
    attended = attended.astype(jnp.bfloat16).reshape(tokens, inner_width)
    own_half, other_half = copies_to_all(attended)
    own_half = own_half.transpose(1, 0, 2).reshape(tokens, -1)
    other_half = other_half.transpose(1, 0, 2).reshape(tokens, -1)
    ratio = lax.axis_size("dp") // lax.axis_size("mp")
    columns = columns.reshape(2, ratio, own_half.shape[1], -1)
    parts = [
        jnp.dot(own_half, columns[0, k], preferred_element_type=jnp.float32)
        + jnp.dot(other_half, columns[1, k], preferred_element_type=jnp.float32)
        for k in range(ratio)
    ]
    return jnp.concatenate(parts, axis=1).astype(jnp.bfloat16)


def solution(mesh):
    in_specs = (
        P("dp", "mp"),
        P("dp", None),
        P(None, "mp"),
        P(None, "mp"),
        P("mp", "dp"),
        P("dp", None),
    )
    out_specs = P("dp", "mp")
    return jax.shard_map(
        on_device, mesh=mesh, in_specs=in_specs, out_specs=out_specs, check_vma=False
    )
```

```python
import math

import jax
import jax.numpy as jnp
from jax import lax
from jax.sharding import PartitionSpec as P

HEAD_DIM = 128
SPAN = 64
NEIGH = 2
NROW = 128
BLK_DEV = 4


NEAR_DP = 8


def weight_blocks(out_weight):
    dp_count = lax.axis_size("dp")
    mp_count = lax.axis_size("mp")
    ratio = dp_count // mp_count
    far_count = dp_count // NEAR_DP
    moves = []
    for d in range(dp_count):
        for m in range(mp_count):
            order = (d % ratio) * mp_count + m
            place = (order % far_count) * NEAR_DP + order // far_count
            moves.append((d * mp_count + m, place * mp_count + d // ratio))
    return lax.ppermute(out_weight, ("dp", "mp"), moves)


def to_far(block):
    dp_count = lax.axis_size("dp")
    groups = [list(range(z, dp_count, NEAR_DP)) for z in range(NEAR_DP)]
    copies = jnp.broadcast_to(block[None], (dp_count // NEAR_DP, *block.shape))
    return lax.all_to_all(
        copies, "dp", split_axis=0, concat_axis=0, axis_index_groups=groups, tiled=True
    )


def to_near(piece):
    dp_count = lax.axis_size("dp")
    groups = [list(range(y, y + NEAR_DP)) for y in range(0, dp_count, NEAR_DP)]
    return lax.all_gather(piece, "dp", axis=0, axis_index_groups=groups, tiled=True)


def copies_to_all(block, axis):
    count = lax.axis_size(axis)
    copies = jnp.broadcast_to(block[None], (count, *block.shape))
    return lax.all_to_all(copies, axis, split_axis=0, concat_axis=0, tiled=True)


def own_part(database):
    mp_count = lax.axis_size("mp")
    part_rows = NROW // mp_count
    enc_width = database.shape[1]
    return lax.dynamic_slice(
        database.reshape(BLK_DEV, NROW, enc_width),
        (0, lax.axis_index("mp") * part_rows, 0),
        (BLK_DEV, part_rows, enc_width),
    )


def near_rows(stored, neighbours):
    far_count, part_rows, enc_width = stored.shape[1], stored.shape[3], stored.shape[4]
    per_owner = neighbours.size
    ids = neighbours.reshape(-1)
    shard_of = ids // BLK_DEV
    place = (shard_of % NEAR_DP * far_count + shard_of // NEAR_DP) * BLK_DEV + ids % BLK_DEV
    stored = stored.reshape(-1, part_rows, enc_width)
    chosen = [
        lax.dynamic_slice(stored, (place[j], 0, 0), (1, part_rows, enc_width))
        for j in range(per_owner)
    ]
    chosen = jnp.concatenate(chosen, axis=0)
    gathered = copies_to_all(chosen, "mp")
    gathered = gathered.reshape(-1, per_owner // NEIGH, NEIGH * part_rows, enc_width)
    return gathered.transpose(1, 0, 2, 3).reshape(-1, enc_width)


def on_device(queries, database, key_weight, value_weight, out_weight, neighbours):
    span_count = neighbours.shape[0]
    inner_width = key_weight.shape[1]
    head_count = inner_width // HEAD_DIM
    mp_count = lax.axis_size("mp")
    moved = weight_blocks(out_weight)
    part = to_far(own_part(database))
    stored = to_near(part[None])
    _, moved = lax.optimization_barrier((part, moved))
    piece = to_far(moved).reshape(-1, moved.shape[1])
    columns = to_near(piece).reshape(-1, mp_count * moved.shape[0], moved.shape[1])
    encoded_rows = near_rows(stored, neighbours)
    near_keys = jnp.dot(encoded_rows, key_weight, preferred_element_type=jnp.float32).astype(
        jnp.bfloat16
    )
    near_values = jnp.dot(encoded_rows, value_weight, preferred_element_type=jnp.float32).astype(
        jnp.bfloat16
    )
    key_blocks = near_keys.reshape(span_count, NEIGH * NROW, head_count, HEAD_DIM)
    value_blocks = near_values.reshape(span_count, NEIGH * NROW, head_count, HEAD_DIM)
    query_blocks = queries.reshape(span_count, SPAN, head_count, HEAD_DIM)
    scores = jnp.einsum(
        "cqhd,ckhd->chqk", query_blocks, key_blocks, preferred_element_type=jnp.float32
    )
    scores = scores / math.sqrt(HEAD_DIM)
    weights = jax.nn.softmax(scores, axis=-1).astype(jnp.bfloat16)
    attended = jnp.einsum(
        "chqk,ckhd->cqhd", weights, value_blocks, preferred_element_type=jnp.float32
    )
    attended = attended.astype(jnp.bfloat16).reshape(span_count * SPAN, inner_width)
    attended = copies_to_all(attended, "mp").transpose(1, 0, 2).reshape(span_count * SPAN, -1)
    parts = [
        jnp.dot(attended, columns[k], preferred_element_type=jnp.float32)
        for k in range(columns.shape[0])
    ]
    return jnp.concatenate(parts, axis=1).astype(jnp.bfloat16)


def solution(mesh):
    in_specs = (
        P("dp", "mp"),
        P("dp", None),
        P(None, "mp"),
        P(None, "mp"),
        P("mp", "dp"),
        P("dp", None),
    )
    out_specs = P("dp", "mp")
    return jax.shard_map(
        on_device, mesh=mesh, in_specs=in_specs, out_specs=out_specs, check_vma=False
    )
```

```python
import math

import jax
import jax.numpy as jnp
from jax import lax
from jax.experimental import pallas as pl
from jax.experimental.pallas import tpu as pltpu
from jax.sharding import PartitionSpec as P

HEAD_DIM = 128
SPAN = 64
NEIGH = 2
NROW = 128
BLK_DEV = 4


NEAR_DP = 8


def far_piece(out_weight):
    dp_count = lax.axis_size("dp")
    mp_count = lax.axis_size("mp")
    ratio = dp_count // mp_count
    far_count = dp_count // NEAR_DP
    blocks = []
    for step in range(far_count):
        moves = []
        for d in range(dp_count):
            for m in range(mp_count):
                order = (d % ratio) * mp_count + m
                place = (order % far_count ^ step) * NEAR_DP + order // far_count
                moves.append((d * mp_count + m, place * mp_count + d // ratio))
        blocks.append(lax.ppermute(out_weight, ("dp", "mp"), moves))
    return blocks


def in_order(blocks):
    far = lax.axis_index("dp") // NEAR_DP
    piece = jnp.zeros((len(blocks), *blocks[0].shape), blocks[0].dtype)
    for step, block in enumerate(blocks):
        piece = lax.dynamic_update_slice(piece, block[None], (far ^ step, 0, 0))
    return piece.reshape(-1, blocks[0].shape[1])


def near_gather(piece):
    dp_count = lax.axis_size("dp")
    groups = [list(range(y, y + NEAR_DP)) for y in range(0, dp_count, NEAR_DP)]
    return lax.all_gather(piece, "dp", axis=0, axis_index_groups=groups, tiled=True)


def pick(indices, blocks, copies):
    def body(indices_ref, blocks_ref, out_ref):
        for j in range(indices.shape[0]):
            block = blocks_ref[indices_ref[j]]
            for c in range(copies):
                out_ref[c, j] = block

    return pl.pallas_call(
        body,
        out_shape=jax.ShapeDtypeStruct((copies, *indices.shape, *blocks.shape[1:]), blocks.dtype),
        in_specs=[
            pl.BlockSpec(memory_space=pltpu.SMEM),
            pl.BlockSpec(memory_space=pltpu.VMEM),
        ],
        out_specs=pl.BlockSpec(memory_space=pltpu.VMEM),
        name="pick",
    )(indices, blocks)


def rows_to_send(database, neighbours):
    dp_count = lax.axis_size("dp")
    part_rows = NROW // lax.axis_size("mp")
    enc_width = database.shape[1]
    flat_ids = neighbours.reshape(1, -1)
    shard_ids = jnp.arange(dp_count, dtype=jnp.int32)[:, None]
    asked = jnp.sum(jnp.where(flat_ids // BLK_DEV == shard_ids, flat_ids % BLK_DEV, 0), axis=1)
    wanted = lax.all_to_all(
        asked.reshape(dp_count, 1), "dp", split_axis=0, concat_axis=0, tiled=True
    ).reshape(dp_count)
    stored = lax.dynamic_slice(
        database.reshape(BLK_DEV, NROW, enc_width),
        (0, lax.axis_index("mp") * part_rows, 0),
        (BLK_DEV, part_rows, enc_width),
    )
    return pick(wanted, stored, 1)[0]


def near_rows(arrived, neighbours):
    mp_count = lax.axis_size("mp")
    part_rows, enc_width = arrived.shape[1:]
    per_owner = neighbours.size
    copies = pick(neighbours.reshape(-1) // BLK_DEV, arrived, mp_count)
    gathered = lax.all_to_all(copies, "mp", split_axis=0, concat_axis=0, tiled=True)
    gathered = gathered.reshape(mp_count, per_owner // NEIGH, NEIGH * part_rows, enc_width)
    return gathered.transpose(1, 0, 2, 3).reshape(-1, enc_width)


def copies_to_all(block, axis):
    count = lax.axis_size(axis)
    copies = jnp.broadcast_to(block[None], (count, *block.shape))
    return lax.all_to_all(copies, axis, split_axis=0, concat_axis=0, tiled=True)


def on_device(queries, database, key_weight, value_weight, out_weight, neighbours):
    span_count = neighbours.shape[0]
    inner_width = key_weight.shape[1]
    head_count = inner_width // HEAD_DIM
    blocks = far_piece(out_weight)
    outgoing = rows_to_send(database, neighbours)
    arrived = lax.all_to_all(outgoing, "dp", split_axis=0, concat_axis=0, tiled=True)
    arrived, blocks = lax.optimization_barrier((arrived, blocks))
    columns = near_gather(in_order(blocks)).reshape(
        -1, lax.axis_size("mp") * out_weight.shape[0], out_weight.shape[1]
    )
    encoded_rows = near_rows(arrived, neighbours)
    near_keys = jnp.dot(encoded_rows, key_weight, preferred_element_type=jnp.float32).astype(
        jnp.bfloat16
    )
    near_values = jnp.dot(encoded_rows, value_weight, preferred_element_type=jnp.float32).astype(
        jnp.bfloat16
    )
    key_blocks = near_keys.reshape(span_count, NEIGH * NROW, head_count, HEAD_DIM)
    value_blocks = near_values.reshape(span_count, NEIGH * NROW, head_count, HEAD_DIM)
    query_blocks = queries.reshape(span_count, SPAN, head_count, HEAD_DIM)
    scores = jnp.einsum(
        "cqhd,ckhd->chqk", query_blocks, key_blocks, preferred_element_type=jnp.float32
    )
    scores = scores / math.sqrt(HEAD_DIM)
    weights = jax.nn.softmax(scores, axis=-1).astype(jnp.bfloat16)
    attended = jnp.einsum(
        "chqk,ckhd->cqhd", weights, value_blocks, preferred_element_type=jnp.float32
    )
    attended = attended.astype(jnp.bfloat16).reshape(span_count * SPAN, inner_width)
    attended = copies_to_all(attended, "mp").transpose(1, 0, 2).reshape(span_count * SPAN, -1)
    parts = [
        jnp.dot(attended, columns[k], preferred_element_type=jnp.float32)
        for k in range(columns.shape[0])
    ]
    return jnp.concatenate(parts, axis=1).astype(jnp.bfloat16)


def solution(mesh):
    in_specs = (
        P("dp", "mp"),
        P("dp", None),
        P(None, "mp"),
        P(None, "mp"),
        P("mp", "dp"),
        P("dp", None),
    )
    out_specs = P("dp", "mp")
    return jax.shard_map(
        on_device, mesh=mesh, in_specs=in_specs, out_specs=out_specs, check_vma=False
    )
```

```python
import math

import jax
import jax.numpy as jnp
from jax import lax
from jax.experimental import pallas as pl
from jax.experimental.pallas import tpu as pltpu
from jax.sharding import PartitionSpec as P

HEAD_DIM = 128
SPAN = 64
NEIGH = 2
NROW = 128
BLK_DEV = 4


NEAR_DP = 8
LOCAL_MP = 4


def weight_block(out_weight):
    dp_count = lax.axis_size("dp")
    mp_count = lax.axis_size("mp")
    moves = []
    for d in range(dp_count):
        for m in range(mp_count):
            near = d % NEAR_DP
            local = m % LOCAL_MP
            ratio = NEAR_DP // LOCAL_MP
            to_near = near % ratio * LOCAL_MP + local
            to_local = near // ratio
            target = (d - near + to_near) * mp_count + m - local + to_local
            moves.append((d * mp_count + m, target))
    return lax.ppermute(out_weight, ("dp", "mp"), moves)


def far_blocks(moved):
    dp_count = lax.axis_size("dp")
    blocks = [moved]
    for step in range(1, dp_count // NEAR_DP):
        pairs = [(d, d ^ (step * NEAR_DP)) for d in range(dp_count)]
        blocks.append(lax.ppermute(moved, "dp", pairs))
    return jnp.stack(blocks)


def near_gather(piece):
    dp_count = lax.axis_size("dp")
    groups = [list(range(y, y + NEAR_DP)) for y in range(0, dp_count, NEAR_DP)]
    return lax.all_gather(piece, "dp", axis=0, axis_index_groups=groups)


def exchange(blocks, groups):
    return lax.all_to_all(
        blocks, "mp", split_axis=0, concat_axis=0, axis_index_groups=groups, tiled=True
    )


def partial_products(attended, columns):
    part_count, local_count, far_count, row_count, width = columns.shape
    tokens = attended.shape[1]
    far = (lax.axis_index("dp") // NEAR_DP).astype(jnp.int32).reshape(1)

    def body(far_ref, attended_ref, columns_ref, out_ref):
        total = jnp.zeros((tokens, width), jnp.float32)
        for local in range(local_count):
            total += jnp.dot(
                attended_ref[local], columns_ref[0, local, 0], preferred_element_type=jnp.float32
            )
        out_ref[0] = total.astype(out_ref.dtype)

    return pl.pallas_call(
        body,
        out_shape=jax.ShapeDtypeStruct((far_count, tokens, part_count * width), attended.dtype),
        grid_spec=pltpu.PrefetchScalarGridSpec(
            num_scalar_prefetch=1,
            grid=(far_count, part_count),
            in_specs=[
                pl.BlockSpec(attended.shape, lambda i, j, far_ref: (0, 0, 0)),
                pl.BlockSpec(
                    (1, local_count, 1, row_count, width),
                    lambda i, j, far_ref: (j, 0, i ^ far_ref[0], 0, 0),
                ),
            ],
            out_specs=pl.BlockSpec((1, tokens, width), lambda i, j, far_ref: (i, 0, j)),
        ),
        cost_estimate=pl.CostEstimate(
            flops=2 * tokens * columns.size,
            bytes_accessed=2 * columns.size,
            transcendentals=0,
        ),
        name="partial_products",
    )(far, attended, columns)


def pick(indices, blocks, copies):
    def body(indices_ref, blocks_ref, out_ref):
        for j in range(indices.shape[0]):
            block = blocks_ref[indices_ref[j]]
            for c in range(copies):
                out_ref[c, j] = block

    return pl.pallas_call(
        body,
        out_shape=jax.ShapeDtypeStruct((copies, *indices.shape, *blocks.shape[1:]), blocks.dtype),
        in_specs=[
            pl.BlockSpec(memory_space=pltpu.SMEM),
            pl.BlockSpec(memory_space=pltpu.VMEM),
        ],
        out_specs=pl.BlockSpec(memory_space=pltpu.VMEM),
        name="pick",
    )(indices, blocks)


def rows_to_send(database, neighbours, piece):
    dp_count = lax.axis_size("dp")
    part_rows = NROW // lax.axis_size("mp")
    enc_width = database.shape[1]
    flat_ids = neighbours.reshape(1, -1)
    shard_ids = jnp.arange(dp_count, dtype=jnp.int32)[:, None]
    asked = jnp.sum(jnp.where(flat_ids // BLK_DEV == shard_ids, flat_ids % BLK_DEV, 0), axis=1)
    wanted = lax.all_to_all(
        asked.reshape(dp_count, 1), "dp", split_axis=0, concat_axis=0, tiled=True
    ).reshape(dp_count)
    stored = lax.dynamic_slice(
        database.reshape(BLK_DEV, NROW, enc_width),
        (0, lax.axis_index("mp") * part_rows, 0),
        (BLK_DEV, part_rows, enc_width),
    )
    wanted, piece = lax.optimization_barrier((wanted, piece))
    return pick(wanted, stored, 1)[0], piece


def near_rows(arrived, neighbours):
    mp_count = lax.axis_size("mp")
    part_rows, enc_width = arrived.shape[1:]
    per_owner = neighbours.size
    copies = pick(neighbours.reshape(-1) // BLK_DEV, arrived, mp_count)
    gathered = lax.all_to_all(copies, "mp", split_axis=0, concat_axis=0, tiled=True)
    gathered = gathered.reshape(mp_count, per_owner // NEIGH, NEIGH * part_rows, enc_width)
    return gathered.transpose(1, 0, 2, 3).reshape(-1, enc_width)


def on_device(queries, database, key_weight, value_weight, out_weight, neighbours):
    span_count = neighbours.shape[0]
    inner_width = key_weight.shape[1]
    head_count = inner_width // HEAD_DIM
    mp_count = lax.axis_size("mp")
    piece = far_blocks(weight_block(out_weight))
    outgoing, piece = rows_to_send(database, neighbours, piece)
    columns = near_gather(piece)
    columns = columns.reshape(-1, LOCAL_MP, *columns.shape[1:])
    arrived = lax.all_to_all(outgoing, "dp", split_axis=0, concat_axis=0, tiled=True)
    encoded_rows = near_rows(arrived, neighbours)
    near_keys = jnp.dot(encoded_rows, key_weight, preferred_element_type=jnp.float32).astype(
        jnp.bfloat16
    )
    near_values = jnp.dot(encoded_rows, value_weight, preferred_element_type=jnp.float32).astype(
        jnp.bfloat16
    )
    key_blocks = near_keys.reshape(span_count, NEIGH * NROW, head_count, HEAD_DIM)
    value_blocks = near_values.reshape(span_count, NEIGH * NROW, head_count, HEAD_DIM)
    query_blocks = queries.reshape(span_count, SPAN, head_count, HEAD_DIM)
    scores = jnp.einsum(
        "cqhd,ckhd->chqk", query_blocks, key_blocks, preferred_element_type=jnp.float32
    )
    scores = scores / math.sqrt(HEAD_DIM)
    weights = jax.nn.softmax(scores, axis=-1).astype(jnp.bfloat16)
    attended = jnp.einsum(
        "chqk,ckhd->cqhd", weights, value_blocks, preferred_element_type=jnp.float32
    )
    attended = attended.astype(jnp.bfloat16).reshape(span_count * SPAN, inner_width)
    copies = jnp.broadcast_to(attended[None], (LOCAL_MP, *attended.shape))
    local_groups = [list(range(m, m + LOCAL_MP)) for m in range(0, mp_count, LOCAL_MP)]
    ring_groups = [list(range(r, mp_count, LOCAL_MP)) for r in range(LOCAL_MP)]
    partials = partial_products(exchange(copies, local_groups), columns)
    partials = exchange(partials, ring_groups).astype(jnp.float32)
    return jnp.sum(partials, axis=0).astype(jnp.bfloat16)


def solution(mesh):
    in_specs = (
        P("dp", "mp"),
        P("dp", None),
        P(None, "mp"),
        P(None, "mp"),
        P("mp", "dp"),
        P("dp", None),
    )
    out_specs = P("dp", "mp")
    return jax.shard_map(
        on_device, mesh=mesh, in_specs=in_specs, out_specs=out_specs, check_vma=False
    )
```

```python
import math

import jax
import jax.numpy as jnp
from jax import lax
from jax.experimental import pallas as pl
from jax.experimental.pallas import tpu as pltpu
from jax.sharding import PartitionSpec as P

HEAD_DIM = 128
SPAN = 64
NEIGH = 2
NROW = 128
BLK_DEV = 4


NEAR_DP = 8
LOCAL_MP = 4
LANES = 128


def weight_block(out_weight):
    dp_count = lax.axis_size("dp")
    mp_count = lax.axis_size("mp")
    moves = []
    for d in range(dp_count):
        for m in range(mp_count):
            near = d % NEAR_DP
            local = m % LOCAL_MP
            ratio = NEAR_DP // LOCAL_MP
            to_near = near % ratio * LOCAL_MP + local
            to_local = near // ratio
            target = (d - near + to_near) * mp_count + m - local + to_local
            moves.append((d * mp_count + m, target))
    return lax.ppermute(out_weight, ("dp", "mp"), moves)


def far_blocks(moved):
    dp_count = lax.axis_size("dp")
    blocks = [moved]
    for step in range(1, dp_count // NEAR_DP):
        pairs = [(d, d ^ (step * NEAR_DP)) for d in range(dp_count)]
        blocks.append(lax.ppermute(moved, "dp", pairs))
    return jnp.stack(blocks)


def near_gather(piece):
    dp_count = lax.axis_size("dp")
    groups = [list(range(y, y + NEAR_DP)) for y in range(0, dp_count, NEAR_DP)]
    return lax.all_gather(piece, "dp", axis=0, axis_index_groups=groups)


def exchange(blocks, groups):
    return lax.all_to_all(
        blocks, "mp", split_axis=0, concat_axis=0, axis_index_groups=groups, tiled=True
    )


def partial_products(attended, columns):
    part_count, local_count, far_count, row_count, width = columns.shape
    tokens = attended.shape[1]
    far = (lax.axis_index("dp") // NEAR_DP).astype(jnp.int32).reshape(1)

    def body(far_ref, attended_ref, columns_ref, out_ref):
        for part in range(part_count):
            total = jnp.zeros((tokens, width), jnp.float32)
            for local in range(local_count):
                total += jnp.dot(
                    attended_ref[local],
                    columns_ref[part, local, 0],
                    preferred_element_type=jnp.float32,
                )
            out_ref[0, :, part * width : (part + 1) * width] = total.astype(out_ref.dtype)

    return pl.pallas_call(
        body,
        out_shape=jax.ShapeDtypeStruct((far_count, tokens, part_count * width), attended.dtype),
        grid_spec=pltpu.PrefetchScalarGridSpec(
            num_scalar_prefetch=1,
            grid=(far_count,),
            in_specs=[
                pl.BlockSpec(attended.shape, lambda i, far_ref: (0, 0, 0)),
                pl.BlockSpec(
                    (part_count, local_count, 1, row_count, width),
                    lambda i, far_ref: (0, 0, i ^ far_ref[0], 0, 0),
                ),
            ],
            out_specs=pl.BlockSpec(
                (1, tokens, part_count * width), lambda i, far_ref: (i, 0, 0)
            ),
        ),
        cost_estimate=pl.CostEstimate(
            flops=2 * tokens * columns.size,
            bytes_accessed=2 * columns.size,
            transcendentals=0,
        ),
        name="partial_products",
    )(far, attended, columns)


def pick(indices, blocks, copies):
    def body(indices_ref, blocks_ref, out_ref):
        for j in range(indices.shape[0]):
            block = blocks_ref[indices_ref[j, 0]]
            for c in range(copies):
                out_ref[c, j] = block

    return pl.pallas_call(
        body,
        out_shape=jax.ShapeDtypeStruct(
            (copies, indices.shape[0], *blocks.shape[1:]), blocks.dtype
        ),
        in_specs=[
            pl.BlockSpec(memory_space=pltpu.SMEM),
            pl.BlockSpec(memory_space=pltpu.VMEM),
        ],
        out_specs=pl.BlockSpec(memory_space=pltpu.VMEM),
        name="pick",
    )(indices, blocks)


def request(neighbours):
    dp_count = lax.axis_size("dp")
    flat_ids = neighbours.reshape(1, -1)
    shard_ids = jnp.arange(dp_count, dtype=jnp.int32)[:, None]
    asked = jnp.sum(jnp.where(flat_ids // BLK_DEV == shard_ids, flat_ids % BLK_DEV, 0), axis=1)
    asked = jnp.broadcast_to(asked[:, None], (dp_count, LANES))
    return lax.all_to_all(asked, "dp", split_axis=0, concat_axis=0, tiled=True)


def rows_to_send(database, wanted):
    part_rows = NROW // lax.axis_size("mp")
    enc_width = database.shape[1]
    stored = lax.dynamic_slice(
        database.reshape(BLK_DEV, NROW, enc_width),
        (0, lax.axis_index("mp") * part_rows, 0),
        (BLK_DEV, part_rows, enc_width),
    )
    return pick(wanted, stored, 1)[0]


def near_rows(arrived, neighbours):
    mp_count = lax.axis_size("mp")
    part_rows, enc_width = arrived.shape[1:]
    per_owner = neighbours.size
    copies = pick(neighbours.reshape(-1, 1) // BLK_DEV, arrived, mp_count)
    gathered = lax.all_to_all(copies, "mp", split_axis=0, concat_axis=0, tiled=True)
    gathered = gathered.reshape(mp_count, per_owner // NEIGH, NEIGH * part_rows, enc_width)
    return gathered.transpose(1, 0, 2, 3).reshape(-1, enc_width)


def on_device(queries, database, key_weight, value_weight, out_weight, neighbours):
    span_count = neighbours.shape[0]
    inner_width = key_weight.shape[1]
    head_count = inner_width // HEAD_DIM
    mp_count = lax.axis_size("mp")
    moved = weight_block(out_weight)
    wanted, moved = lax.optimization_barrier((request(neighbours), moved))
    wanted, piece = lax.optimization_barrier((wanted, far_blocks(moved)))
    outgoing = rows_to_send(database, wanted)
    columns = near_gather(piece)
    columns = columns.reshape(-1, LOCAL_MP, *columns.shape[1:])
    arrived = lax.all_to_all(outgoing, "dp", split_axis=0, concat_axis=0, tiled=True)
    encoded_rows = near_rows(arrived, neighbours)
    near_keys = jnp.dot(encoded_rows, key_weight, preferred_element_type=jnp.float32).astype(
        jnp.bfloat16
    )
    near_values = jnp.dot(encoded_rows, value_weight, preferred_element_type=jnp.float32).astype(
        jnp.bfloat16
    )
    key_blocks = near_keys.reshape(span_count, NEIGH * NROW, head_count, HEAD_DIM)
    value_blocks = near_values.reshape(span_count, NEIGH * NROW, head_count, HEAD_DIM)
    query_blocks = queries.reshape(span_count, SPAN, head_count, HEAD_DIM)
    scores = jnp.einsum(
        "cqhd,ckhd->chqk", query_blocks, key_blocks, preferred_element_type=jnp.float32
    )
    scores = scores / math.sqrt(HEAD_DIM)
    weights = jax.nn.softmax(scores, axis=-1).astype(jnp.bfloat16)
    attended = jnp.einsum(
        "chqk,ckhd->cqhd", weights, value_blocks, preferred_element_type=jnp.float32
    )
    attended = attended.astype(jnp.bfloat16).reshape(span_count * SPAN, inner_width)
    copies = jnp.broadcast_to(attended[None], (LOCAL_MP, *attended.shape))
    local_groups = [list(range(m, m + LOCAL_MP)) for m in range(0, mp_count, LOCAL_MP)]
    ring_groups = [list(range(r, mp_count, LOCAL_MP)) for r in range(LOCAL_MP)]
    partials = partial_products(exchange(copies, local_groups), columns)
    partials = exchange(partials, ring_groups).astype(jnp.float32)
    return jnp.sum(partials, axis=0).astype(jnp.bfloat16)


def solution(mesh):
    in_specs = (
        P("dp", "mp"),
        P("dp", None),
        P(None, "mp"),
        P(None, "mp"),
        P("mp", "dp"),
        P("dp", None),
    )
    out_specs = P("dp", "mp")
    return jax.shard_map(
        on_device, mesh=mesh, in_specs=in_specs, out_specs=out_specs, check_vma=False
    )
```

```python
import math

import jax
import jax.numpy as jnp
from jax import lax
from jax.experimental import pallas as pl
from jax.experimental.pallas import tpu as pltpu
from jax.sharding import PartitionSpec as P

HEAD_DIM = 128
SPAN = 64
NEIGH = 2
NROW = 128
BLK_DEV = 4


NEAR_DP = 8
LANES = 128


def weight_block(out_weight):
    dp_count = lax.axis_size("dp")
    mp_count = lax.axis_size("mp")
    ratio = dp_count // mp_count
    far_count = dp_count // NEAR_DP
    moves = []
    for d in range(dp_count):
        for m in range(mp_count):
            near = d % ratio * (mp_count // far_count) + m // far_count
            place = m % far_count * NEAR_DP + near
            moves.append((d * mp_count + m, place * mp_count + d // ratio))
    return lax.ppermute(out_weight, ("dp", "mp"), moves)


def far_blocks(moved):
    dp_count = lax.axis_size("dp")
    blocks = [moved]
    for step in range(1, dp_count // NEAR_DP):
        pairs = [(d, d ^ (step * NEAR_DP)) for d in range(dp_count)]
        blocks.append(lax.ppermute(moved, "dp", pairs))
    return jnp.stack(blocks)


def near_gather(piece):
    dp_count = lax.axis_size("dp")
    groups = [list(range(y, y + NEAR_DP)) for y in range(0, dp_count, NEAR_DP)]
    return lax.all_gather(piece, "dp", axis=0, axis_index_groups=groups)


def product(attended, columns):
    part_count, outer_count, far_count, row_count, width = columns.shape
    tokens = attended.shape[1]
    far = (lax.axis_index("dp") // NEAR_DP).astype(jnp.int32).reshape(1)

    def body(far_ref, attended_ref, columns_ref, out_ref, total_ref):
        outer = pl.program_id(0)
        parts = [jnp.zeros((tokens, width), jnp.float32) for _ in range(part_count)]
        for slot in range(far_count):
            block = attended_ref[outer * far_count + (slot ^ far_ref[0])]
            for part in range(part_count):
                parts[part] += jnp.dot(
                    block, columns_ref[part, 0, slot], preferred_element_type=jnp.float32
                )
        for part in range(part_count):
            lanes = slice(part * width, (part + 1) * width)

            @pl.when(outer == 0)
            def _():
                total_ref[:, lanes] = parts[part]

            @pl.when(outer > 0)
            def _():
                total_ref[:, lanes] += parts[part]

        @pl.when(outer == outer_count - 1)
        def _():
            out_ref[...] = total_ref[...].astype(out_ref.dtype)

    return pl.pallas_call(
        body,
        out_shape=jax.ShapeDtypeStruct((tokens, part_count * width), attended.dtype),
        grid_spec=pltpu.PrefetchScalarGridSpec(
            num_scalar_prefetch=1,
            grid=(outer_count,),
            in_specs=[
                pl.BlockSpec(attended.shape, lambda i, far_ref: (0, 0, 0)),
                pl.BlockSpec(
                    (part_count, 1, far_count, row_count, width),
                    lambda i, far_ref: (0, i, 0, 0, 0),
                ),
            ],
            out_specs=pl.BlockSpec((tokens, part_count * width), lambda i, far_ref: (0, 0)),
            scratch_shapes=[pltpu.VMEM((tokens, part_count * width), jnp.float32)],
        ),
        cost_estimate=pl.CostEstimate(
            flops=2 * tokens * columns.size,
            bytes_accessed=2 * columns.size,
            transcendentals=0,
        ),
        name="product",
    )(far, attended, columns)


def pick(indices, blocks, copies):
    def body(indices_ref, blocks_ref, out_ref):
        for j in range(indices.shape[0]):
            block = blocks_ref[indices_ref[j, 0]]
            for c in range(copies):
                out_ref[c, j] = block

    return pl.pallas_call(
        body,
        out_shape=jax.ShapeDtypeStruct(
            (copies, indices.shape[0], *blocks.shape[1:]), blocks.dtype
        ),
        in_specs=[
            pl.BlockSpec(memory_space=pltpu.SMEM),
            pl.BlockSpec(memory_space=pltpu.VMEM),
        ],
        out_specs=pl.BlockSpec(memory_space=pltpu.VMEM),
        name="pick",
    )(indices, blocks)


def request(neighbours):
    dp_count = lax.axis_size("dp")
    flat_ids = neighbours.reshape(1, -1)
    shard_ids = jnp.arange(dp_count, dtype=jnp.int32)[:, None]
    asked = jnp.sum(jnp.where(flat_ids // BLK_DEV == shard_ids, flat_ids % BLK_DEV, 0), axis=1)
    asked = jnp.broadcast_to(asked[:, None], (dp_count, LANES))
    return lax.all_to_all(asked, "dp", split_axis=0, concat_axis=0, tiled=True)


def rows_to_send(database, wanted):
    part_rows = NROW // lax.axis_size("mp")
    enc_width = database.shape[1]
    stored = lax.dynamic_slice(
        database.reshape(BLK_DEV, NROW, enc_width),
        (0, lax.axis_index("mp") * part_rows, 0),
        (BLK_DEV, part_rows, enc_width),
    )
    return pick(wanted, stored, 1)[0]


def near_rows(arrived, neighbours):
    mp_count = lax.axis_size("mp")
    part_rows, enc_width = arrived.shape[1:]
    per_owner = neighbours.size
    copies = pick(neighbours.reshape(-1, 1) // BLK_DEV, arrived, mp_count)
    gathered = lax.all_to_all(copies, "mp", split_axis=0, concat_axis=0, tiled=True)
    gathered = gathered.reshape(mp_count, per_owner // NEIGH, NEIGH * part_rows, enc_width)
    return gathered.transpose(1, 0, 2, 3).reshape(-1, enc_width)


def on_device(queries, database, key_weight, value_weight, out_weight, neighbours):
    span_count = neighbours.shape[0]
    inner_width = key_weight.shape[1]
    head_count = inner_width // HEAD_DIM
    mp_count = lax.axis_size("mp")
    moved = weight_block(out_weight)
    wanted, _ = lax.optimization_barrier((request(neighbours), moved))
    outgoing = rows_to_send(database, wanted)
    arrived = lax.all_to_all(outgoing, "dp", split_axis=0, concat_axis=0, tiled=True)
    arrived, piece = lax.optimization_barrier((arrived, far_blocks(moved)))
    columns = near_gather(piece)
    ratio = lax.axis_size("dp") // mp_count
    columns = columns.reshape(ratio, -1, *columns.shape[1:])
    encoded_rows = near_rows(arrived, neighbours)
    near_keys = jnp.dot(encoded_rows, key_weight, preferred_element_type=jnp.float32).astype(
        jnp.bfloat16
    )
    near_values = jnp.dot(encoded_rows, value_weight, preferred_element_type=jnp.float32).astype(
        jnp.bfloat16
    )
    key_blocks = near_keys.reshape(span_count, NEIGH * NROW, head_count, HEAD_DIM)
    value_blocks = near_values.reshape(span_count, NEIGH * NROW, head_count, HEAD_DIM)
    query_blocks = queries.reshape(span_count, SPAN, head_count, HEAD_DIM)
    scores = jnp.einsum(
        "cqhd,ckhd->chqk", query_blocks, key_blocks, preferred_element_type=jnp.float32
    )
    scores = scores / math.sqrt(HEAD_DIM)
    weights = jax.nn.softmax(scores, axis=-1).astype(jnp.bfloat16)
    attended = jnp.einsum(
        "chqk,ckhd->cqhd", weights, value_blocks, preferred_element_type=jnp.float32
    )
    attended = attended.astype(jnp.bfloat16).reshape(span_count * SPAN, inner_width)
    copies = jnp.broadcast_to(attended[None], (mp_count, *attended.shape))
    attended = lax.all_to_all(copies, "mp", split_axis=0, concat_axis=0, tiled=True)
    return product(attended, columns)


def solution(mesh):
    in_specs = (
        P("dp", "mp"),
        P("dp", None),
        P(None, "mp"),
        P(None, "mp"),
        P("mp", "dp"),
        P("dp", None),
    )
    out_specs = P("dp", "mp")
    return jax.shard_map(
        on_device, mesh=mesh, in_specs=in_specs, out_specs=out_specs, check_vma=False
    )
```

```python
import math

import jax
import jax.numpy as jnp
from jax import lax
from jax.experimental import pallas as pl
from jax.experimental.pallas import tpu as pltpu
from jax.sharding import PartitionSpec as P

HEAD_DIM = 128
SPAN = 64
NEIGH = 2
NROW = 128
BLK_DEV = 4


NEAR_DP = 8
LANES = 128


def weight_block(out_weight):
    dp_count = lax.axis_size("dp")
    mp_count = lax.axis_size("mp")
    ratio = dp_count // mp_count
    far_count = dp_count // NEAR_DP
    moves = []
    for d in range(dp_count):
        for m in range(mp_count):
            near = d % ratio * (mp_count // far_count) + m // far_count
            place = m % far_count * NEAR_DP + near
            moves.append((d * mp_count + m, place * mp_count + d // ratio))
    return lax.ppermute(out_weight, ("dp", "mp"), moves)


def far_blocks(moved):
    dp_count = lax.axis_size("dp")
    blocks = [moved]
    for step in range(1, dp_count // NEAR_DP):
        pairs = [(d, d ^ (step * NEAR_DP)) for d in range(dp_count)]
        blocks.append(lax.ppermute(moved, "dp", pairs))
    return jnp.stack(blocks)


def near_gather(piece):
    dp_count = lax.axis_size("dp")
    groups = [list(range(y, y + NEAR_DP)) for y in range(0, dp_count, NEAR_DP)]
    return lax.all_gather(piece, "dp", axis=0, axis_index_groups=groups)


def product(attended, columns):
    part_count, outer_count, far_count, row_count, width = columns.shape
    tokens = attended.shape[1]
    far = (lax.axis_index("dp") // NEAR_DP).astype(jnp.int32).reshape(1)

    def body(far_ref, attended_ref, columns_ref, out_ref, total_ref):
        outer = pl.program_id(0)
        parts = [jnp.zeros((tokens, width), jnp.float32) for _ in range(part_count)]
        for slot in range(far_count):
            block = attended_ref[outer * far_count + (slot ^ far_ref[0])]
            for part in range(part_count):
                parts[part] += jnp.dot(
                    block, columns_ref[part, 0, slot], preferred_element_type=jnp.float32
                )
        for part in range(part_count):
            lanes = slice(part * width, (part + 1) * width)

            @pl.when(outer == 0)
            def _():
                total_ref[:, lanes] = parts[part]

            @pl.when(outer > 0)
            def _():
                total_ref[:, lanes] += parts[part]

        @pl.when(outer == outer_count - 1)
        def _():
            out_ref[...] = total_ref[...].astype(out_ref.dtype)

    return pl.pallas_call(
        body,
        out_shape=jax.ShapeDtypeStruct((tokens, part_count * width), attended.dtype),
        grid_spec=pltpu.PrefetchScalarGridSpec(
            num_scalar_prefetch=1,
            grid=(outer_count,),
            in_specs=[
                pl.BlockSpec(attended.shape, lambda i, far_ref: (0, 0, 0)),
                pl.BlockSpec(
                    (part_count, 1, far_count, row_count, width),
                    lambda i, far_ref: (0, i, 0, 0, 0),
                ),
            ],
            out_specs=pl.BlockSpec((tokens, part_count * width), lambda i, far_ref: (0, 0)),
            scratch_shapes=[pltpu.VMEM((tokens, part_count * width), jnp.float32)],
        ),
        cost_estimate=pl.CostEstimate(
            flops=2 * tokens * columns.size,
            bytes_accessed=2 * columns.size,
            transcendentals=0,
        ),
        name="product",
    )(far, attended, columns)


def pick(indices, blocks, copies):
    def body(indices_ref, blocks_ref, out_ref):
        for j in range(indices.shape[0]):
            block = blocks_ref[indices_ref[j, 0]]
            for c in range(copies):
                out_ref[c, j] = block

    return pl.pallas_call(
        body,
        out_shape=jax.ShapeDtypeStruct(
            (copies, indices.shape[0], *blocks.shape[1:]), blocks.dtype
        ),
        in_specs=[
            pl.BlockSpec(memory_space=pltpu.SMEM),
            pl.BlockSpec(memory_space=pltpu.VMEM),
        ],
        out_specs=pl.BlockSpec(memory_space=pltpu.VMEM),
        name="pick",
    )(indices, blocks)


def request(neighbours):
    dp_count = lax.axis_size("dp")
    flat_ids = neighbours.reshape(1, -1)
    shard_ids = jnp.arange(dp_count, dtype=jnp.int32)[:, None]
    asked = jnp.sum(jnp.where(flat_ids // BLK_DEV == shard_ids, flat_ids % BLK_DEV, 0), axis=1)
    asked = jnp.broadcast_to(asked[:, None], (dp_count, LANES))
    return lax.all_to_all(asked, "dp", split_axis=0, concat_axis=0, tiled=True)


def rows_to_send(database, wanted):
    part_rows = NROW // lax.axis_size("mp")
    enc_width = database.shape[1]
    stored = lax.dynamic_slice(
        database.reshape(BLK_DEV, NROW, enc_width),
        (0, lax.axis_index("mp") * part_rows, 0),
        (BLK_DEV, part_rows, enc_width),
    )
    return pick(wanted, stored, 1)[0]


def near_rows(arrived, neighbours):
    mp_count = lax.axis_size("mp")
    copies = pick(neighbours.reshape(-1, 1) // BLK_DEV, arrived, mp_count)
    return lax.all_to_all(copies, "mp", split_axis=0, concat_axis=0, tiled=True)


def attend(rows, queries, key_weight, value_weight, copies):
    source_count, block_count, part_rows, enc_width = rows.shape
    tokens, inner_width = queries.shape
    span_count = tokens // SPAN
    span_rows = NEIGH * part_rows
    scale = 1.0 / math.sqrt(HEAD_DIM)

    def body(rows_ref, queries_ref, key_ref, value_ref, out_ref, encoded_ref):
        for source in range(source_count):
            for block in range(block_count):
                span, place = divmod(block, NEIGH)
                start = (span * source_count + source) * span_rows + place * part_rows
                encoded_ref[start : start + part_rows] = rows_ref[source, block]
        encoded = encoded_ref[...]
        keys = jnp.dot(encoded, key_ref[...], preferred_element_type=jnp.float32)
        keys = keys.astype(jnp.bfloat16)
        values = jnp.dot(encoded, value_ref[...], preferred_element_type=jnp.float32)
        values = values.astype(jnp.bfloat16)
        for span in range(span_count):
            own = slice(span * NEIGH * NROW, (span + 1) * NEIGH * NROW)
            own_tokens = slice(span * SPAN, (span + 1) * SPAN)
            for head in range(inner_width // HEAD_DIM):
                lanes = slice(head * HEAD_DIM, (head + 1) * HEAD_DIM)
                scores = lax.dot_general(
                    queries_ref[own_tokens, lanes],
                    keys[own, lanes],
                    (((1,), (1,)), ((), ())),
                    preferred_element_type=jnp.float32,
                )
                scores = scores * scale
                weights = jnp.exp(scores - jnp.max(scores, axis=-1, keepdims=True))
                weights = weights / jnp.sum(weights, axis=-1, keepdims=True)
                result = jnp.dot(
                    weights.astype(jnp.bfloat16),
                    values[own, lanes],
                    preferred_element_type=jnp.float32,
                ).astype(out_ref.dtype)
                for copy in range(copies):
                    out_ref[copy, own_tokens, lanes] = result

    return pl.pallas_call(
        body,
        out_shape=jax.ShapeDtypeStruct((copies, tokens, inner_width), jnp.bfloat16),
        in_specs=[pl.BlockSpec(memory_space=pltpu.VMEM)] * 4,
        out_specs=pl.BlockSpec(memory_space=pltpu.VMEM),
        scratch_shapes=[pltpu.VMEM((block_count * NROW, enc_width), jnp.bfloat16)],
        cost_estimate=pl.CostEstimate(
            flops=4 * block_count * NROW * enc_width * inner_width,
            bytes_accessed=2 * (rows.size + 2 * key_weight.size + copies * queries.size),
            transcendentals=span_count * SPAN * NEIGH * NROW * inner_width // HEAD_DIM,
        ),
        name="attend",
    )(rows, queries, key_weight, value_weight)


def on_device(queries, database, key_weight, value_weight, out_weight, neighbours):
    mp_count = lax.axis_size("mp")
    moved = weight_block(out_weight)
    outgoing = rows_to_send(database, request(neighbours))
    outgoing, _ = lax.optimization_barrier((outgoing, moved))
    arrived = lax.all_to_all(outgoing, "dp", split_axis=0, concat_axis=0, tiled=True)
    arrived, piece = lax.optimization_barrier((arrived, far_blocks(moved)))
    columns = near_gather(piece)
    ratio = lax.axis_size("dp") // mp_count
    columns = columns.reshape(ratio, -1, *columns.shape[1:])
    rows = near_rows(arrived, neighbours)
    copies = attend(rows, queries, key_weight, value_weight, mp_count)
    attended = lax.all_to_all(copies, "mp", split_axis=0, concat_axis=0, tiled=True)
    return product(attended, columns)


def solution(mesh):
    in_specs = (
        P("dp", "mp"),
        P("dp", None),
        P(None, "mp"),
        P(None, "mp"),
        P("mp", "dp"),
        P("dp", None),
    )
    out_specs = P("dp", "mp")
    return jax.shard_map(
        on_device, mesh=mesh, in_specs=in_specs, out_specs=out_specs, check_vma=False
    )
```

```python
import math

import jax
import jax.numpy as jnp
from jax import lax
from jax.experimental import pallas as pl
from jax.experimental.pallas import tpu as pltpu
from jax.sharding import PartitionSpec as P

HEAD_DIM = 128
SPAN = 64
NEIGH = 2
NROW = 128
BLK_DEV = 4


NEAR_DP = 8
LOCAL_MP = 4
LANES = 128


def far_blocks(out_weight):
    dp_count = lax.axis_size("dp")
    mp_count = lax.axis_size("mp")
    ratio = NEAR_DP // LOCAL_MP
    blocks = []
    for step in range(dp_count // NEAR_DP):
        moves = []
        for d in range(dp_count):
            for m in range(mp_count):
                near = d % NEAR_DP
                local = m % LOCAL_MP
                to_near = near % ratio * LOCAL_MP + local
                to_d = (d - near) ^ (step * NEAR_DP) | to_near
                moves.append((d * mp_count + m, to_d * mp_count + m - local + near // ratio))
        blocks.append(lax.ppermute(out_weight, ("dp", "mp"), moves))
    return jnp.stack(blocks)


def near_gather(piece):
    dp_count = lax.axis_size("dp")
    groups = [list(range(y, y + NEAR_DP)) for y in range(0, dp_count, NEAR_DP)]
    return lax.all_gather(piece, "dp", axis=0, axis_index_groups=groups)


def exchange(blocks, groups):
    return lax.all_to_all(
        blocks, "mp", split_axis=0, concat_axis=0, axis_index_groups=groups, tiled=True
    )


def partial_products(attended, columns):
    part_count, local_count, far_count, row_count, width = columns.shape
    tokens = attended.shape[1]
    far = (lax.axis_index("dp") // NEAR_DP).astype(jnp.int32).reshape(1)

    def body(far_ref, attended_ref, columns_ref, out_ref):
        for part in range(part_count):
            total = jnp.zeros((tokens, width), jnp.float32)
            for local in range(local_count):
                total += jnp.dot(
                    attended_ref[local],
                    columns_ref[part, local, 0],
                    preferred_element_type=jnp.float32,
                )
            out_ref[0, :, part * width : (part + 1) * width] = total.astype(out_ref.dtype)

    return pl.pallas_call(
        body,
        out_shape=jax.ShapeDtypeStruct((far_count, tokens, part_count * width), attended.dtype),
        grid_spec=pltpu.PrefetchScalarGridSpec(
            num_scalar_prefetch=1,
            grid=(far_count,),
            in_specs=[
                pl.BlockSpec(attended.shape, lambda i, far_ref: (0, 0, 0)),
                pl.BlockSpec(
                    (part_count, local_count, 1, row_count, width),
                    lambda i, far_ref: (0, 0, i ^ far_ref[0], 0, 0),
                ),
            ],
            out_specs=pl.BlockSpec(
                (1, tokens, part_count * width), lambda i, far_ref: (i, 0, 0)
            ),
        ),
        cost_estimate=pl.CostEstimate(
            flops=2 * tokens * columns.size,
            bytes_accessed=2 * columns.size,
            transcendentals=0,
        ),
        name="partial_products",
    )(far, attended, columns)


def pick(indices, blocks, copies):
    def body(indices_ref, blocks_ref, out_ref):
        for j in range(indices.shape[0]):
            block = blocks_ref[indices_ref[j, 0]]
            for c in range(copies):
                out_ref[c, j] = block

    return pl.pallas_call(
        body,
        out_shape=jax.ShapeDtypeStruct(
            (copies, indices.shape[0], *blocks.shape[1:]), blocks.dtype
        ),
        in_specs=[
            pl.BlockSpec(memory_space=pltpu.SMEM),
            pl.BlockSpec(memory_space=pltpu.VMEM),
        ],
        out_specs=pl.BlockSpec(memory_space=pltpu.VMEM),
        name="pick",
    )(indices, blocks)


def request(neighbours):
    dp_count = lax.axis_size("dp")
    flat_ids = neighbours.reshape(1, -1)
    shard_ids = jnp.arange(dp_count, dtype=jnp.int32)[:, None]
    asked = jnp.sum(jnp.where(flat_ids // BLK_DEV == shard_ids, flat_ids % BLK_DEV, 0), axis=1)
    asked = jnp.broadcast_to(asked[:, None], (dp_count, LANES))
    return lax.all_to_all(asked, "dp", split_axis=0, concat_axis=0, tiled=True)


def rows_to_send(database, wanted):
    part_rows = NROW // lax.axis_size("mp")
    enc_width = database.shape[1]
    stored = lax.dynamic_slice(
        database.reshape(BLK_DEV, NROW, enc_width),
        (0, lax.axis_index("mp") * part_rows, 0),
        (BLK_DEV, part_rows, enc_width),
    )
    return pick(wanted, stored, 1)[0]


def near_rows(arrived, neighbours):
    mp_count = lax.axis_size("mp")
    copies = pick(neighbours.reshape(-1, 1) // BLK_DEV, arrived, mp_count)
    return lax.all_to_all(copies, "mp", split_axis=0, concat_axis=0, tiled=True)


def attend(rows, queries, key_weight, value_weight, copies):
    source_count, block_count, part_rows, enc_width = rows.shape
    tokens, inner_width = queries.shape
    span_count = tokens // SPAN
    span_rows = NEIGH * part_rows
    scale = 1.0 / math.sqrt(HEAD_DIM)

    def body(rows_ref, queries_ref, key_ref, value_ref, out_ref, encoded_ref):
        for source in range(source_count):
            for block in range(block_count):
                span, place = divmod(block, NEIGH)
                start = (span * source_count + source) * span_rows + place * part_rows
                encoded_ref[start : start + part_rows] = rows_ref[source, block]
        encoded = encoded_ref[...]
        keys = jnp.dot(encoded, key_ref[...], preferred_element_type=jnp.float32)
        keys = keys.astype(jnp.bfloat16)
        values = jnp.dot(encoded, value_ref[...], preferred_element_type=jnp.float32)
        values = values.astype(jnp.bfloat16)
        for span in range(span_count):
            own = slice(span * NEIGH * NROW, (span + 1) * NEIGH * NROW)
            own_tokens = slice(span * SPAN, (span + 1) * SPAN)
            for head in range(inner_width // HEAD_DIM):
                lanes = slice(head * HEAD_DIM, (head + 1) * HEAD_DIM)
                scores = lax.dot_general(
                    queries_ref[own_tokens, lanes],
                    keys[own, lanes],
                    (((1,), (1,)), ((), ())),
                    preferred_element_type=jnp.float32,
                )
                scores = scores * scale
                weights = jnp.exp(scores - jnp.max(scores, axis=-1, keepdims=True))
                weights = weights / jnp.sum(weights, axis=-1, keepdims=True)
                result = jnp.dot(
                    weights.astype(jnp.bfloat16),
                    values[own, lanes],
                    preferred_element_type=jnp.float32,
                ).astype(out_ref.dtype)
                for copy in range(copies):
                    out_ref[copy, own_tokens, lanes] = result

    return pl.pallas_call(
        body,
        out_shape=jax.ShapeDtypeStruct((copies, tokens, inner_width), jnp.bfloat16),
        in_specs=[pl.BlockSpec(memory_space=pltpu.VMEM)] * 4,
        out_specs=pl.BlockSpec(memory_space=pltpu.VMEM),
        scratch_shapes=[pltpu.VMEM((block_count * NROW, enc_width), jnp.bfloat16)],
        cost_estimate=pl.CostEstimate(
            flops=4 * block_count * NROW * enc_width * inner_width,
            bytes_accessed=2 * (rows.size + 2 * key_weight.size + copies * queries.size),
            transcendentals=span_count * SPAN * NEIGH * NROW * inner_width // HEAD_DIM,
        ),
        name="attend",
    )(rows, queries, key_weight, value_weight)


def on_device(queries, database, key_weight, value_weight, out_weight, neighbours):
    mp_count = lax.axis_size("mp")
    wanted, piece = lax.optimization_barrier((request(neighbours), far_blocks(out_weight)))
    outgoing = rows_to_send(database, wanted)
    columns = near_gather(piece)
    columns = columns.reshape(-1, LOCAL_MP, *columns.shape[1:])
    arrived = lax.all_to_all(outgoing, "dp", split_axis=0, concat_axis=0, tiled=True)
    rows = near_rows(arrived, neighbours)
    copies = attend(rows, queries, key_weight, value_weight, LOCAL_MP)
    local_groups = [list(range(m, m + LOCAL_MP)) for m in range(0, mp_count, LOCAL_MP)]
    ring_groups = [list(range(r, mp_count, LOCAL_MP)) for r in range(LOCAL_MP)]
    partials = partial_products(exchange(copies, local_groups), columns)
    partials = exchange(partials, ring_groups).astype(jnp.float32)
    return jnp.sum(partials, axis=0).astype(jnp.bfloat16)


def solution(mesh):
    in_specs = (
        P("dp", "mp"),
        P("dp", None),
        P(None, "mp"),
        P(None, "mp"),
        P("mp", "dp"),
        P("dp", None),
    )
    out_specs = P("dp", "mp")
    return jax.shard_map(
        on_device, mesh=mesh, in_specs=in_specs, out_specs=out_specs, check_vma=False
    )
```

```python
import math

import jax
import jax.numpy as jnp
from jax import lax
from jax.experimental import pallas as pl
from jax.experimental.pallas import tpu as pltpu
from jax.sharding import PartitionSpec as P

HEAD_DIM = 128
SPAN = 64
NEIGH = 2
NROW = 128
BLK_DEV = 4


NEAR_DP = 8
LOCAL_MP = 4
LANES = 128


def weight_block(out_weight):
    dp_count = lax.axis_size("dp")
    mp_count = lax.axis_size("mp")
    moves = []
    for d in range(dp_count):
        for m in range(mp_count):
            near = d % NEAR_DP
            local = m % LOCAL_MP
            ratio = NEAR_DP // LOCAL_MP
            to_near = near % ratio * LOCAL_MP + local
            to_local = near // ratio
            target = (d - near + to_near) * mp_count + m - local + to_local
            moves.append((d * mp_count + m, target))
    return lax.ppermute(out_weight, ("dp", "mp"), moves)


def far_blocks(moved):
    dp_count = lax.axis_size("dp")
    blocks = [moved]
    for step in range(1, dp_count // NEAR_DP):
        pairs = [(d, d ^ (step * NEAR_DP)) for d in range(dp_count)]
        blocks.append(lax.ppermute(moved, "dp", pairs))
    return jnp.stack(blocks)


def near_gather(piece):
    dp_count = lax.axis_size("dp")
    groups = [list(range(y, y + NEAR_DP)) for y in range(0, dp_count, NEAR_DP)]
    return lax.all_gather(piece, "dp", axis=0, axis_index_groups=groups)


def exchange(blocks, groups):
    return lax.all_to_all(
        blocks, "mp", split_axis=0, concat_axis=0, axis_index_groups=groups, tiled=True
    )


def partial_products(attended, columns):
    part_count, local_count, far_count, row_count, width = columns.shape
    tokens = attended.shape[1]
    far = (lax.axis_index("dp") // NEAR_DP).astype(jnp.int32).reshape(1)

    def body(far_ref, attended_ref, columns_ref, out_ref):
        for part in range(part_count):
            total = jnp.zeros((tokens, width), jnp.float32)
            for local in range(local_count):
                total += jnp.dot(
                    attended_ref[local],
                    columns_ref[part, local, 0],
                    preferred_element_type=jnp.float32,
                )
            out_ref[0, :, part * width : (part + 1) * width] = total.astype(out_ref.dtype)

    return pl.pallas_call(
        body,
        out_shape=jax.ShapeDtypeStruct((far_count, tokens, part_count * width), attended.dtype),
        grid_spec=pltpu.PrefetchScalarGridSpec(
            num_scalar_prefetch=1,
            grid=(far_count,),
            in_specs=[
                pl.BlockSpec(attended.shape, lambda i, far_ref: (0, 0, 0)),
                pl.BlockSpec(
                    (part_count, local_count, 1, row_count, width),
                    lambda i, far_ref: (0, 0, i ^ far_ref[0], 0, 0),
                ),
            ],
            out_specs=pl.BlockSpec(
                (1, tokens, part_count * width), lambda i, far_ref: (i, 0, 0)
            ),
        ),
        cost_estimate=pl.CostEstimate(
            flops=2 * tokens * columns.size,
            bytes_accessed=2 * columns.size,
            transcendentals=0,
        ),
        name="partial_products",
    )(far, attended, columns)


def pick(indices, blocks, copies):
    def body(indices_ref, blocks_ref, out_ref):
        for j in range(indices.shape[0]):
            block = blocks_ref[indices_ref[j, 0]]
            for c in range(copies):
                out_ref[c, j] = block

    return pl.pallas_call(
        body,
        out_shape=jax.ShapeDtypeStruct(
            (copies, indices.shape[0], *blocks.shape[1:]), blocks.dtype
        ),
        in_specs=[
            pl.BlockSpec(memory_space=pltpu.SMEM),
            pl.BlockSpec(memory_space=pltpu.VMEM),
        ],
        out_specs=pl.BlockSpec(memory_space=pltpu.VMEM),
        name="pick",
    )(indices, blocks)


def request(neighbours):
    dp_count = lax.axis_size("dp")
    flat_ids = neighbours.reshape(1, -1)
    shard_ids = jnp.arange(dp_count, dtype=jnp.int32)[:, None]
    asked = jnp.sum(jnp.where(flat_ids // BLK_DEV == shard_ids, flat_ids % BLK_DEV, 0), axis=1)
    asked = jnp.broadcast_to(asked[:, None], (dp_count, LANES))
    return lax.all_to_all(asked, "dp", split_axis=0, concat_axis=0, tiled=True)


def rows_to_send(database, wanted):
    part_rows = NROW // lax.axis_size("mp")
    enc_width = database.shape[1]
    stored = lax.dynamic_slice(
        database.reshape(BLK_DEV, NROW, enc_width),
        (0, lax.axis_index("mp") * part_rows, 0),
        (BLK_DEV, part_rows, enc_width),
    )
    return pick(wanted, stored, 1)[0]


def near_rows(arrived, neighbours):
    mp_count = lax.axis_size("mp")
    copies = pick(neighbours.reshape(-1, 1) // BLK_DEV, arrived, mp_count)
    return lax.all_to_all(copies, "mp", split_axis=0, concat_axis=0, tiled=True)


def attend(rows, queries, key_weight, value_weight, copies):
    source_count, block_count, part_rows, enc_width = rows.shape
    tokens, inner_width = queries.shape
    span_count = tokens // SPAN
    span_rows = NEIGH * part_rows
    scale = 1.0 / math.sqrt(HEAD_DIM)

    def body(rows_ref, queries_ref, key_ref, value_ref, out_ref, encoded_ref):
        for source in range(source_count):
            for block in range(block_count):
                span, place = divmod(block, NEIGH)
                start = (span * source_count + source) * span_rows + place * part_rows
                encoded_ref[start : start + part_rows] = rows_ref[source, block]
        encoded = encoded_ref[...]
        keys = jnp.dot(encoded, key_ref[...], preferred_element_type=jnp.float32)
        keys = keys.astype(jnp.bfloat16)
        values = jnp.dot(encoded, value_ref[...], preferred_element_type=jnp.float32)
        values = values.astype(jnp.bfloat16)
        for span in range(span_count):
            own = slice(span * NEIGH * NROW, (span + 1) * NEIGH * NROW)
            own_tokens = slice(span * SPAN, (span + 1) * SPAN)
            for head in range(inner_width // HEAD_DIM):
                lanes = slice(head * HEAD_DIM, (head + 1) * HEAD_DIM)
                scores = lax.dot_general(
                    queries_ref[own_tokens, lanes],
                    keys[own, lanes],
                    (((1,), (1,)), ((), ())),
                    preferred_element_type=jnp.float32,
                )
                scores = scores * scale
                weights = jnp.exp(scores - jnp.max(scores, axis=-1, keepdims=True))
                weights = weights / jnp.sum(weights, axis=-1, keepdims=True)
                result = jnp.dot(
                    weights.astype(jnp.bfloat16),
                    values[own, lanes],
                    preferred_element_type=jnp.float32,
                ).astype(out_ref.dtype)
                for copy in range(copies):
                    out_ref[copy, own_tokens, lanes] = result

    return pl.pallas_call(
        body,
        out_shape=jax.ShapeDtypeStruct((copies, tokens, inner_width), jnp.bfloat16),
        in_specs=[pl.BlockSpec(memory_space=pltpu.VMEM)] * 4,
        out_specs=pl.BlockSpec(memory_space=pltpu.VMEM),
        scratch_shapes=[pltpu.VMEM((block_count * NROW, enc_width), jnp.bfloat16)],
        cost_estimate=pl.CostEstimate(
            flops=4 * block_count * NROW * enc_width * inner_width,
            bytes_accessed=2 * (rows.size + 2 * key_weight.size + copies * queries.size),
            transcendentals=span_count * SPAN * NEIGH * NROW * inner_width // HEAD_DIM,
        ),
        name="attend",
    )(rows, queries, key_weight, value_weight)


def on_device(queries, database, key_weight, value_weight, out_weight, neighbours):
    mp_count = lax.axis_size("mp")
    moved = weight_block(out_weight)
    outgoing = rows_to_send(database, request(neighbours))
    outgoing, _ = lax.optimization_barrier((outgoing, moved))
    arrived = lax.all_to_all(outgoing, "dp", split_axis=0, concat_axis=0, tiled=True)
    arrived, piece = lax.optimization_barrier((arrived, far_blocks(moved)))
    columns = near_gather(piece)
    columns = columns.reshape(-1, LOCAL_MP, *columns.shape[1:])
    rows = near_rows(arrived, neighbours)
    copies = attend(rows, queries, key_weight, value_weight, LOCAL_MP)
    local_groups = [list(range(m, m + LOCAL_MP)) for m in range(0, mp_count, LOCAL_MP)]
    ring_groups = [list(range(r, mp_count, LOCAL_MP)) for r in range(LOCAL_MP)]
    partials = partial_products(exchange(copies, local_groups), columns)
    partials = exchange(partials, ring_groups).astype(jnp.float32)
    return jnp.sum(partials, axis=0).astype(jnp.bfloat16)


def solution(mesh):
    in_specs = (
        P("dp", "mp"),
        P("dp", None),
        P(None, "mp"),
        P(None, "mp"),
        P("mp", "dp"),
        P("dp", None),
    )
    out_specs = P("dp", "mp")
    return jax.shard_map(
        on_device, mesh=mesh, in_specs=in_specs, out_specs=out_specs, check_vma=False
    )
```

```python
import math

import jax
import jax.numpy as jnp
from jax import lax
from jax.experimental import pallas as pl
from jax.experimental.pallas import tpu as pltpu
from jax.sharding import PartitionSpec as P

HEAD_DIM = 128
SPAN = 64
NEIGH = 2
NROW = 128
BLK_DEV = 4


NEAR_DP = 8
LOCAL_MP = 4
LANES = 128


def weight_block(out_weight):
    dp_count = lax.axis_size("dp")
    mp_count = lax.axis_size("mp")
    moves = []
    for d in range(dp_count):
        for m in range(mp_count):
            near = d % NEAR_DP
            local = m % LOCAL_MP
            ratio = NEAR_DP // LOCAL_MP
            to_near = near % ratio * LOCAL_MP + local
            to_local = near // ratio
            target = (d - near + to_near) * mp_count + m - local + to_local
            moves.append((d * mp_count + m, target))
    return lax.ppermute(out_weight, ("dp", "mp"), moves)


def far_blocks(moved):
    dp_count = lax.axis_size("dp")
    blocks = [moved]
    for step in range(1, dp_count // NEAR_DP):
        pairs = [(d, d ^ (step * NEAR_DP)) for d in range(dp_count)]
        blocks.append(lax.ppermute(moved, "dp", pairs))
    return jnp.stack(blocks)


def near_gather(piece):
    dp_count = lax.axis_size("dp")
    groups = [list(range(y, y + NEAR_DP)) for y in range(0, dp_count, NEAR_DP)]
    return lax.all_gather(piece, "dp", axis=0, axis_index_groups=groups)


def exchange(blocks, groups):
    return lax.all_to_all(
        blocks, "mp", split_axis=0, concat_axis=0, axis_index_groups=groups, tiled=True
    )


def partial_products(attended, columns):
    part_count, local_count, far_count, row_count, width = columns.shape
    tokens = attended.shape[1]
    far = (lax.axis_index("dp") // NEAR_DP).astype(jnp.int32).reshape(1)

    def body(far_ref, attended_ref, columns_ref, out_ref):
        for part in range(part_count):
            total = jnp.zeros((tokens, width), jnp.float32)
            for local in range(local_count):
                total += jnp.dot(
                    attended_ref[local],
                    columns_ref[part, local, 0],
                    preferred_element_type=jnp.float32,
                )
            out_ref[0, :, part * width : (part + 1) * width] = total.astype(out_ref.dtype)

    return pl.pallas_call(
        body,
        out_shape=jax.ShapeDtypeStruct((far_count, tokens, part_count * width), attended.dtype),
        grid_spec=pltpu.PrefetchScalarGridSpec(
            num_scalar_prefetch=1,
            grid=(far_count,),
            in_specs=[
                pl.BlockSpec(attended.shape, lambda i, far_ref: (0, 0, 0)),
                pl.BlockSpec(
                    (part_count, local_count, 1, row_count, width),
                    lambda i, far_ref: (0, 0, i ^ far_ref[0], 0, 0),
                ),
            ],
            out_specs=pl.BlockSpec(
                (1, tokens, part_count * width), lambda i, far_ref: (i, 0, 0)
            ),
        ),
        cost_estimate=pl.CostEstimate(
            flops=2 * tokens * columns.size,
            bytes_accessed=2 * columns.size,
            transcendentals=0,
        ),
        name="partial_products",
    )(far, attended, columns)


def pick(indices, blocks, copies):
    def body(indices_ref, blocks_ref, out_ref):
        for j in range(indices.shape[0]):
            block = blocks_ref[indices_ref[j, 0]]
            for c in range(copies):
                out_ref[c, j] = block

    return pl.pallas_call(
        body,
        out_shape=jax.ShapeDtypeStruct(
            (copies, indices.shape[0], *blocks.shape[1:]), blocks.dtype
        ),
        in_specs=[
            pl.BlockSpec(memory_space=pltpu.SMEM),
            pl.BlockSpec(memory_space=pltpu.VMEM),
        ],
        out_specs=pl.BlockSpec(memory_space=pltpu.VMEM),
        name="pick",
    )(indices, blocks)


def request(neighbours):
    dp_count = lax.axis_size("dp")
    flat_ids = neighbours.reshape(1, -1)
    shard_ids = jnp.arange(dp_count, dtype=jnp.int32)[:, None]
    asked = jnp.sum(jnp.where(flat_ids // BLK_DEV == shard_ids, flat_ids % BLK_DEV, 0), axis=1)
    asked = jnp.broadcast_to(asked[:, None], (dp_count, LANES))
    return lax.all_to_all(asked, "dp", split_axis=0, concat_axis=0, tiled=True)


def rows_to_send(database, wanted):
    part_rows = NROW // lax.axis_size("mp")
    enc_width = database.shape[1]
    stored = lax.dynamic_slice(
        database.reshape(BLK_DEV, NROW, enc_width),
        (0, lax.axis_index("mp") * part_rows, 0),
        (BLK_DEV, part_rows, enc_width),
    )
    wanted = wanted[:, :1].reshape(-1, 1, 1)
    outgoing = stored[0][None]
    for block in range(1, BLK_DEV):
        outgoing = jnp.where(wanted == block, stored[block][None], outgoing)
    return jnp.broadcast_to(outgoing, (wanted.shape[0], part_rows, enc_width))


def near_rows(arrived, neighbours):
    mp_count = lax.axis_size("mp")
    copies = pick(neighbours.reshape(-1, 1) // BLK_DEV, arrived, mp_count)
    return lax.all_to_all(copies, "mp", split_axis=0, concat_axis=0, tiled=True)


def attend(rows, queries, key_weight, value_weight, copies):
    source_count, block_count, part_rows, enc_width = rows.shape
    tokens, inner_width = queries.shape
    span_count = tokens // SPAN
    span_rows = NEIGH * part_rows
    scale = 1.0 / math.sqrt(HEAD_DIM)

    def body(rows_ref, queries_ref, key_ref, value_ref, out_ref, encoded_ref):
        for source in range(source_count):
            for block in range(block_count):
                span, place = divmod(block, NEIGH)
                start = (span * source_count + source) * span_rows + place * part_rows
                encoded_ref[start : start + part_rows] = rows_ref[source, block]
        encoded = encoded_ref[...]
        keys = jnp.dot(encoded, key_ref[...], preferred_element_type=jnp.float32)
        keys = keys.astype(jnp.bfloat16)
        values = jnp.dot(encoded, value_ref[...], preferred_element_type=jnp.float32)
        values = values.astype(jnp.bfloat16)
        for span in range(span_count):
            own = slice(span * NEIGH * NROW, (span + 1) * NEIGH * NROW)
            own_tokens = slice(span * SPAN, (span + 1) * SPAN)
            for head in range(inner_width // HEAD_DIM):
                lanes = slice(head * HEAD_DIM, (head + 1) * HEAD_DIM)
                scores = lax.dot_general(
                    queries_ref[own_tokens, lanes],
                    keys[own, lanes],
                    (((1,), (1,)), ((), ())),
                    preferred_element_type=jnp.float32,
                )
                scores = scores * scale
                weights = jnp.exp(scores - jnp.max(scores, axis=-1, keepdims=True))
                weights = weights / jnp.sum(weights, axis=-1, keepdims=True)
                result = jnp.dot(
                    weights.astype(jnp.bfloat16),
                    values[own, lanes],
                    preferred_element_type=jnp.float32,
                ).astype(out_ref.dtype)
                for copy in range(copies):
                    out_ref[copy, own_tokens, lanes] = result

    return pl.pallas_call(
        body,
        out_shape=jax.ShapeDtypeStruct((copies, tokens, inner_width), jnp.bfloat16),
        in_specs=[pl.BlockSpec(memory_space=pltpu.VMEM)] * 4,
        out_specs=pl.BlockSpec(memory_space=pltpu.VMEM),
        scratch_shapes=[pltpu.VMEM((block_count * NROW, enc_width), jnp.bfloat16)],
        cost_estimate=pl.CostEstimate(
            flops=4 * block_count * NROW * enc_width * inner_width,
            bytes_accessed=2 * (rows.size + 2 * key_weight.size + copies * queries.size),
            transcendentals=span_count * SPAN * NEIGH * NROW * inner_width // HEAD_DIM,
        ),
        name="attend",
    )(rows, queries, key_weight, value_weight)


def on_device(queries, database, key_weight, value_weight, out_weight, neighbours):
    mp_count = lax.axis_size("mp")
    moved = weight_block(out_weight)
    outgoing = rows_to_send(database, request(neighbours))
    outgoing, _ = lax.optimization_barrier((outgoing, moved))
    arrived = lax.all_to_all(outgoing, "dp", split_axis=0, concat_axis=0, tiled=True)
    arrived, piece = lax.optimization_barrier((arrived, far_blocks(moved)))
    columns = near_gather(piece)
    columns = columns.reshape(-1, LOCAL_MP, *columns.shape[1:])
    rows = near_rows(arrived, neighbours)
    copies = attend(rows, queries, key_weight, value_weight, LOCAL_MP)
    local_groups = [list(range(m, m + LOCAL_MP)) for m in range(0, mp_count, LOCAL_MP)]
    ring_groups = [list(range(r, mp_count, LOCAL_MP)) for r in range(LOCAL_MP)]
    partials = partial_products(exchange(copies, local_groups), columns)
    partials = exchange(partials, ring_groups).astype(jnp.float32)
    return jnp.sum(partials, axis=0).astype(jnp.bfloat16)


def solution(mesh):
    in_specs = (
        P("dp", "mp"),
        P("dp", None),
        P(None, "mp"),
        P(None, "mp"),
        P("mp", "dp"),
        P("dp", None),
    )
    out_specs = P("dp", "mp")
    return jax.shard_map(
        on_device, mesh=mesh, in_specs=in_specs, out_specs=out_specs, check_vma=False
    )
```

```python
import math

import jax
import jax.numpy as jnp
from jax import lax
from jax.experimental import pallas as pl
from jax.experimental.pallas import tpu as pltpu
from jax.sharding import PartitionSpec as P

HEAD_DIM = 128
SPAN = 64
NEIGH = 2
NROW = 128
BLK_DEV = 4


NEAR_DP = 8
LOCAL_MP = 4
LANES = 128


def weight_block(out_weight):
    dp_count = lax.axis_size("dp")
    mp_count = lax.axis_size("mp")
    moves = []
    for d in range(dp_count):
        for m in range(mp_count):
            near = d % NEAR_DP
            local = m % LOCAL_MP
            ratio = NEAR_DP // LOCAL_MP
            to_near = near % ratio * LOCAL_MP + local
            to_local = near // ratio
            target = (d - near + to_near) * mp_count + m - local + to_local
            moves.append((d * mp_count + m, target))
    return lax.ppermute(out_weight, ("dp", "mp"), moves)


def far_blocks(moved):
    dp_count = lax.axis_size("dp")
    blocks = [moved]
    for step in range(1, dp_count // NEAR_DP):
        pairs = [(d, d ^ (step * NEAR_DP)) for d in range(dp_count)]
        blocks.append(lax.ppermute(moved, "dp", pairs))
    return jnp.stack(blocks)


def near_gather(piece):
    dp_count = lax.axis_size("dp")
    groups = [list(range(y, y + NEAR_DP)) for y in range(0, dp_count, NEAR_DP)]
    return lax.all_gather(piece, "dp", axis=0, axis_index_groups=groups)


def exchange(blocks, groups):
    return lax.all_to_all(
        blocks, "mp", split_axis=0, concat_axis=0, axis_index_groups=groups, tiled=True
    )


def partial_products(attended, columns):
    part_count, local_count, far_count, row_count, width = columns.shape
    tokens = attended.shape[1]
    far = (lax.axis_index("dp") // NEAR_DP).astype(jnp.int32).reshape(1)

    def body(far_ref, attended_ref, columns_ref, out_ref):
        for part in range(part_count):
            total = jnp.zeros((tokens, width), jnp.float32)
            for local in range(local_count):
                total += jnp.dot(
                    attended_ref[local],
                    columns_ref[part, local, 0],
                    preferred_element_type=jnp.float32,
                )
            out_ref[0, :, part * width : (part + 1) * width] = total.astype(out_ref.dtype)

    return pl.pallas_call(
        body,
        out_shape=jax.ShapeDtypeStruct((far_count, tokens, part_count * width), attended.dtype),
        grid_spec=pltpu.PrefetchScalarGridSpec(
            num_scalar_prefetch=1,
            grid=(far_count,),
            in_specs=[
                pl.BlockSpec(attended.shape, lambda i, far_ref: (0, 0, 0)),
                pl.BlockSpec(
                    (part_count, local_count, 1, row_count, width),
                    lambda i, far_ref: (0, 0, i ^ far_ref[0], 0, 0),
                ),
            ],
            out_specs=pl.BlockSpec(
                (1, tokens, part_count * width), lambda i, far_ref: (i, 0, 0)
            ),
        ),
        cost_estimate=pl.CostEstimate(
            flops=2 * tokens * columns.size,
            bytes_accessed=2 * columns.size,
            transcendentals=0,
        ),
        name="partial_products",
    )(far, attended, columns)


def pick(indices, blocks, copies):
    def body(indices_ref, blocks_ref, out_ref):
        for j in range(indices.shape[0]):
            block = blocks_ref[indices_ref[j, 0]]
            for c in range(copies):
                out_ref[c, j] = block

    return pl.pallas_call(
        body,
        out_shape=jax.ShapeDtypeStruct(
            (copies, indices.shape[0], *blocks.shape[1:]), blocks.dtype
        ),
        in_specs=[
            pl.BlockSpec(memory_space=pltpu.SMEM),
            pl.BlockSpec(memory_space=pltpu.VMEM),
        ],
        out_specs=pl.BlockSpec(memory_space=pltpu.VMEM),
        name="pick",
    )(indices, blocks)


def request(neighbours):
    dp_count = lax.axis_size("dp")
    flat_ids = neighbours.reshape(1, -1)
    shard_ids = jnp.arange(dp_count, dtype=jnp.int32)[:, None]
    asked = jnp.sum(jnp.where(flat_ids // BLK_DEV == shard_ids, flat_ids % BLK_DEV, 0), axis=1)
    asked = jnp.broadcast_to(asked[:, None], (dp_count, LANES))
    return lax.all_to_all(asked, "dp", split_axis=0, concat_axis=0, tiled=True)


def rows_to_send(database, wanted):
    part_rows = NROW // lax.axis_size("mp")
    enc_width = database.shape[1]
    stored = lax.dynamic_slice(
        database.reshape(BLK_DEV, NROW, enc_width),
        (0, lax.axis_index("mp") * part_rows, 0),
        (BLK_DEV, part_rows, enc_width),
    )
    wanted = wanted[:, :1].reshape(-1, 1, 1)
    outgoing = stored[0][None]
    for block in range(1, BLK_DEV):
        outgoing = jnp.where(wanted == block, stored[block][None], outgoing)
    return jnp.broadcast_to(outgoing, (wanted.shape[0], part_rows, enc_width))


def near_rows(arrived, neighbours):
    mp_count = lax.axis_size("mp")
    copies = pick(neighbours.reshape(-1, 1) // BLK_DEV, arrived, mp_count)
    return lax.all_to_all(copies, "mp", split_axis=0, concat_axis=0, tiled=True)


def attend(rows, queries, key_weight, value_weight, copies):
    source_count, block_count, part_rows, enc_width = rows.shape
    tokens, inner_width = queries.shape
    span_count = tokens // SPAN
    span_rows = NEIGH * part_rows
    scale = 1.0 / math.sqrt(HEAD_DIM)

    def body(rows_ref, queries_ref, key_ref, value_ref, out_ref, encoded_ref):
        for source in range(source_count):
            for block in range(block_count):
                span, place = divmod(block, NEIGH)
                start = (span * source_count + source) * span_rows + place * part_rows
                encoded_ref[start : start + part_rows] = rows_ref[source, block]
        encoded = encoded_ref[...]
        keys = jnp.dot(encoded, key_ref[...], preferred_element_type=jnp.float32)
        keys = keys.astype(jnp.bfloat16)
        values = jnp.dot(encoded, value_ref[...], preferred_element_type=jnp.float32)
        values = values.astype(jnp.bfloat16)
        for span in range(span_count):
            own = slice(span * NEIGH * NROW, (span + 1) * NEIGH * NROW)
            own_tokens = slice(span * SPAN, (span + 1) * SPAN)
            for head in range(inner_width // HEAD_DIM):
                lanes = slice(head * HEAD_DIM, (head + 1) * HEAD_DIM)
                scores = lax.dot_general(
                    queries_ref[own_tokens, lanes],
                    keys[own, lanes],
                    (((1,), (1,)), ((), ())),
                    preferred_element_type=jnp.float32,
                )
                scores = scores * scale
                weights = jnp.exp(scores - jnp.max(scores, axis=-1, keepdims=True))
                weights = weights / jnp.sum(weights, axis=-1, keepdims=True)
                result = jnp.dot(
                    weights.astype(jnp.bfloat16),
                    values[own, lanes],
                    preferred_element_type=jnp.float32,
                ).astype(out_ref.dtype)
                for copy in range(copies):
                    out_ref[copy, own_tokens, lanes] = result

    return pl.pallas_call(
        body,
        out_shape=jax.ShapeDtypeStruct((copies, tokens, inner_width), jnp.bfloat16),
        in_specs=[pl.BlockSpec(memory_space=pltpu.VMEM)] * 4,
        out_specs=pl.BlockSpec(memory_space=pltpu.VMEM),
        scratch_shapes=[pltpu.VMEM((block_count * NROW, enc_width), jnp.bfloat16)],
        cost_estimate=pl.CostEstimate(
            flops=4 * block_count * NROW * enc_width * inner_width,
            bytes_accessed=2 * (rows.size + 2 * key_weight.size + copies * queries.size),
            transcendentals=span_count * SPAN * NEIGH * NROW * inner_width // HEAD_DIM,
        ),
        name="attend",
    )(rows, queries, key_weight, value_weight)


def on_device(queries, database, key_weight, value_weight, out_weight, neighbours):
    mp_count = lax.axis_size("mp")
    moved = weight_block(out_weight)
    outgoing = rows_to_send(database, request(neighbours))
    arrived = lax.all_to_all(outgoing, "dp", split_axis=0, concat_axis=0, tiled=True)
    arrived, piece = lax.optimization_barrier((arrived, far_blocks(moved)))
    columns = near_gather(piece)
    columns = columns.reshape(-1, LOCAL_MP, *columns.shape[1:])
    rows = near_rows(arrived, neighbours)
    copies = attend(rows, queries, key_weight, value_weight, LOCAL_MP)
    local_groups = [list(range(m, m + LOCAL_MP)) for m in range(0, mp_count, LOCAL_MP)]
    ring_groups = [list(range(r, mp_count, LOCAL_MP)) for r in range(LOCAL_MP)]
    partials = partial_products(exchange(copies, local_groups), columns)
    partials = exchange(partials, ring_groups).astype(jnp.float32)
    return jnp.sum(partials, axis=0).astype(jnp.bfloat16)


def solution(mesh):
    in_specs = (
        P("dp", "mp"),
        P("dp", None),
        P(None, "mp"),
        P(None, "mp"),
        P("mp", "dp"),
        P("dp", None),
    )
    out_specs = P("dp", "mp")
    return jax.shard_map(
        on_device, mesh=mesh, in_specs=in_specs, out_specs=out_specs, check_vma=False
    )
```

```python
import math

import jax
import jax.numpy as jnp
from jax import lax
from jax.experimental import pallas as pl
from jax.experimental.pallas import tpu as pltpu
from jax.sharding import PartitionSpec as P

HEAD_DIM = 128
SPAN = 64
NEIGH = 2
NROW = 128
BLK_DEV = 4


NEAR_DP = 8
LOCAL_MP = 4
LANES = 128


def weight_block(out_weight):
    dp_count = lax.axis_size("dp")
    mp_count = lax.axis_size("mp")
    moves = []
    for d in range(dp_count):
        for m in range(mp_count):
            near = d % NEAR_DP
            local = m % LOCAL_MP
            ratio = NEAR_DP // LOCAL_MP
            to_near = near % ratio * LOCAL_MP + local
            to_local = near // ratio
            target = (d - near + to_near) * mp_count + m - local + to_local
            moves.append((d * mp_count + m, target))
    return lax.ppermute(out_weight, ("dp", "mp"), moves)


def far_blocks(moved):
    dp_count = lax.axis_size("dp")
    blocks = {0: moved}
    for step in sorted(range(1, dp_count // NEAR_DP), key=lambda k: (k != 2, k)):
        pairs = [(d, d ^ (step * NEAR_DP)) for d in range(dp_count)]
        blocks[step] = lax.ppermute(moved, "dp", pairs)
    return jnp.stack([blocks[k] for k in sorted(blocks)])


def near_gather(piece):
    dp_count = lax.axis_size("dp")
    groups = [list(range(y, y + NEAR_DP)) for y in range(0, dp_count, NEAR_DP)]
    return lax.all_gather(piece, "dp", axis=0, axis_index_groups=groups)


def exchange(blocks, groups):
    return lax.all_to_all(
        blocks, "mp", split_axis=0, concat_axis=0, axis_index_groups=groups, tiled=True
    )


def partial_products(attended, columns):
    part_count, local_count, far_count, row_count, width = columns.shape
    tokens = attended.shape[1]
    far = (lax.axis_index("dp") // NEAR_DP).astype(jnp.int32).reshape(1)

    def body(far_ref, attended_ref, columns_ref, out_ref):
        for part in range(part_count):
            total = jnp.zeros((tokens, width), jnp.float32)
            for local in range(local_count):
                total += jnp.dot(
                    attended_ref[local],
                    columns_ref[part, local, 0],
                    preferred_element_type=jnp.float32,
                )
            out_ref[0, :, part * width : (part + 1) * width] = total.astype(out_ref.dtype)

    return pl.pallas_call(
        body,
        out_shape=jax.ShapeDtypeStruct((far_count, tokens, part_count * width), attended.dtype),
        grid_spec=pltpu.PrefetchScalarGridSpec(
            num_scalar_prefetch=1,
            grid=(far_count,),
            in_specs=[
                pl.BlockSpec(attended.shape, lambda i, far_ref: (0, 0, 0)),
                pl.BlockSpec(
                    (part_count, local_count, 1, row_count, width),
                    lambda i, far_ref: (0, 0, i ^ far_ref[0], 0, 0),
                ),
            ],
            out_specs=pl.BlockSpec(
                (1, tokens, part_count * width), lambda i, far_ref: (i, 0, 0)
            ),
        ),
        cost_estimate=pl.CostEstimate(
            flops=2 * tokens * columns.size,
            bytes_accessed=2 * columns.size,
            transcendentals=0,
        ),
        name="partial_products",
    )(far, attended, columns)


def pick(indices, blocks, copies):
    def body(indices_ref, blocks_ref, out_ref):
        for j in range(indices.shape[0]):
            block = blocks_ref[indices_ref[j, 0]]
            for c in range(copies):
                out_ref[c, j] = block

    return pl.pallas_call(
        body,
        out_shape=jax.ShapeDtypeStruct(
            (copies, indices.shape[0], *blocks.shape[1:]), blocks.dtype
        ),
        in_specs=[
            pl.BlockSpec(memory_space=pltpu.SMEM),
            pl.BlockSpec(memory_space=pltpu.VMEM),
        ],
        out_specs=pl.BlockSpec(memory_space=pltpu.VMEM),
        name="pick",
    )(indices, blocks)


def request(neighbours):
    dp_count = lax.axis_size("dp")
    flat_ids = neighbours.reshape(1, -1)
    shard_ids = jnp.arange(dp_count, dtype=jnp.int32)[:, None]
    asked = jnp.sum(jnp.where(flat_ids // BLK_DEV == shard_ids, flat_ids % BLK_DEV, 0), axis=1)
    asked = jnp.broadcast_to(asked[:, None], (dp_count, LANES))
    return lax.all_to_all(asked, "dp", split_axis=0, concat_axis=0, tiled=True)


def rows_to_send(database, wanted):
    part_rows = NROW // lax.axis_size("mp")
    enc_width = database.shape[1]
    stored = lax.dynamic_slice(
        database.reshape(BLK_DEV, NROW, enc_width),
        (0, lax.axis_index("mp") * part_rows, 0),
        (BLK_DEV, part_rows, enc_width),
    )
    return pick(wanted, stored, 1)[0]


def near_rows(arrived, neighbours):
    mp_count = lax.axis_size("mp")
    copies = pick(neighbours.reshape(-1, 1) // BLK_DEV, arrived, mp_count)
    return lax.all_to_all(copies, "mp", split_axis=0, concat_axis=0, tiled=True)


def attend(rows, queries, key_weight, value_weight, copies):
    source_count, block_count, part_rows, enc_width = rows.shape
    tokens, inner_width = queries.shape
    span_count = tokens // SPAN
    span_rows = NEIGH * part_rows
    scale = 1.0 / math.sqrt(HEAD_DIM)

    def body(rows_ref, queries_ref, key_ref, value_ref, out_ref, encoded_ref):
        for source in range(source_count):
            for block in range(block_count):
                span, place = divmod(block, NEIGH)
                start = (span * source_count + source) * span_rows + place * part_rows
                encoded_ref[start : start + part_rows] = rows_ref[source, block]
        encoded = encoded_ref[...]
        keys = jnp.dot(encoded, key_ref[...], preferred_element_type=jnp.float32)
        keys = keys.astype(jnp.bfloat16)
        values = jnp.dot(encoded, value_ref[...], preferred_element_type=jnp.float32)
        values = values.astype(jnp.bfloat16)
        for span in range(span_count):
            own = slice(span * NEIGH * NROW, (span + 1) * NEIGH * NROW)
            own_tokens = slice(span * SPAN, (span + 1) * SPAN)
            for head in range(inner_width // HEAD_DIM):
                lanes = slice(head * HEAD_DIM, (head + 1) * HEAD_DIM)
                scores = lax.dot_general(
                    queries_ref[own_tokens, lanes],
                    keys[own, lanes],
                    (((1,), (1,)), ((), ())),
                    preferred_element_type=jnp.float32,
                )
                scores = scores * scale
                weights = jnp.exp(scores - jnp.max(scores, axis=-1, keepdims=True))
                weights = weights / jnp.sum(weights, axis=-1, keepdims=True)
                result = jnp.dot(
                    weights.astype(jnp.bfloat16),
                    values[own, lanes],
                    preferred_element_type=jnp.float32,
                ).astype(out_ref.dtype)
                for copy in range(copies):
                    out_ref[copy, own_tokens, lanes] = result

    return pl.pallas_call(
        body,
        out_shape=jax.ShapeDtypeStruct((copies, tokens, inner_width), jnp.bfloat16),
        in_specs=[pl.BlockSpec(memory_space=pltpu.VMEM)] * 4,
        out_specs=pl.BlockSpec(memory_space=pltpu.VMEM),
        scratch_shapes=[pltpu.VMEM((block_count * NROW, enc_width), jnp.bfloat16)],
        cost_estimate=pl.CostEstimate(
            flops=4 * block_count * NROW * enc_width * inner_width,
            bytes_accessed=2 * (rows.size + 2 * key_weight.size + copies * queries.size),
            transcendentals=span_count * SPAN * NEIGH * NROW * inner_width // HEAD_DIM,
        ),
        name="attend",
    )(rows, queries, key_weight, value_weight)


def on_device(queries, database, key_weight, value_weight, out_weight, neighbours):
    mp_count = lax.axis_size("mp")
    moved = weight_block(out_weight)
    outgoing = rows_to_send(database, request(neighbours))
    outgoing, _ = lax.optimization_barrier((outgoing, moved))
    arrived = lax.all_to_all(outgoing, "dp", split_axis=0, concat_axis=0, tiled=True)
    arrived, piece = lax.optimization_barrier((arrived, far_blocks(moved)))
    columns = near_gather(piece)
    columns = columns.reshape(-1, LOCAL_MP, *columns.shape[1:])
    rows = near_rows(arrived, neighbours)
    copies = attend(rows, queries, key_weight, value_weight, LOCAL_MP)
    local_groups = [list(range(m, m + LOCAL_MP)) for m in range(0, mp_count, LOCAL_MP)]
    ring_groups = [list(range(r, mp_count, LOCAL_MP)) for r in range(LOCAL_MP)]
    partials = partial_products(exchange(copies, local_groups), columns)
    partials = exchange(partials, ring_groups).astype(jnp.float32)
    return jnp.sum(partials, axis=0).astype(jnp.bfloat16)


def solution(mesh):
    in_specs = (
        P("dp", "mp"),
        P("dp", None),
        P(None, "mp"),
        P(None, "mp"),
        P("mp", "dp"),
        P("dp", None),
    )
    out_specs = P("dp", "mp")
    return jax.shard_map(
        on_device, mesh=mesh, in_specs=in_specs, out_specs=out_specs, check_vma=False
    )
```
